256 devices in a mesh: row: 16 (over z, core), col: 16 (over x, y).
Axes of the slice: x: 4, y: 4, z: 8, core: 2. Of those that a mesh axis runs over, the one named last changes fastest.
Arguments:
- inputs: bfloat16 [3, 64, 128, 2048], P(None, None, 'row', 'col'), may hold values from -6 to 6
- gate_pre: bfloat16 [3, 256, 128, 2048], P(None, None, 'row', 'col'), may hold values from -8 to 8
- cotangent: bfloat16 [3, 64, 128, 2048], P(None, None, 'row', 'col'), may hold values from -6 to 6
- hidden_init: bfloat16 [64, 128, 2048], P(None, 'row', 'col'), may hold values from -6 to 6
- cell_init: float32 [64, 128, 2048], P(None, 'row', 'col'), may hold values from -6 to 6
- land_mask: int32 [128, 2048], P('row', 'col'), may hold values 0 or 1
- kernel: bfloat16 [256, 1152], replicated, may hold values from -0.1875 to 0.1875
Outputs:
- grad_inputs: bfloat16 [3, 64, 128, 2048], P(None, None, 'row', 'col')
- grad_hidden: float32 [64, 128, 2048], P(None, 'row', 'col')
- grad_cell: float32 [64, 128, 2048], P(None, 'row', 'col')
- grad_kernel: float32 [256, 1152], P('row', 'col')
- grad_bias: float32 [256], P(('row', 'col'))
The draws below stay inside these ranges and needn't reach their ends.
Inputs may be any that keep to these rules, and one draw needn't show every extreme that they name: `land_mask`: 1 marks a land cell.
All inputs are finite; a program needn't handle non-finite values. No bound on the sum of `land_mask` on one device may be relied on, other than what follows from the above.
Results may differ from the reference program's by a relative error of at most 0.005.
Values may be sent and summed in bfloat16 or wider, within the bound.
No kernel may reach another device: no remote copies, remote signals or barrier semaphores. Data moves between devices by JAX's collectives and lax.ppermute only.
A program may use at most 64 MiB of HBM per device.

```python
import jax
import jax.numpy as jnp
from jax import lax

IN = 64
HID = 64
STEPS = 3
NH = 128
NW = 2048
GATES = 256
TAPS = 1152


def place_ends(result, own_key, smallest, largest):
    index_at = [jax.random.randint(jax.random.fold_in(own_key, axis), (), 0, length) for axis, length in enumerate(result.shape)]
    main_axis = result.shape.index(max(result.shape))
    beside = index_at[:main_axis] + [(index_at[main_axis] + 1) % result.shape[main_axis]] + index_at[main_axis + 1:]
    return result.at[tuple(index_at)].set(smallest).at[tuple(beside)].set(largest)


def block_scale(key, shape, pieces, low, top_value):
    gain = 1.0
    for position, shards_of in pieces:
        steps = jax.random.uniform(jax.random.fold_in(jax.random.fold_in(key, 6), position), (shards_of,), jnp.float32, low / len(pieces), top_value / len(pieces))
        gain = gain * jnp.repeat(jnp.exp(steps), shape[position] // shards_of).reshape((-1,) + (1,) * (len(shape) - 1 - position))
    return gain


def scatter_about(stream_key, shape, spread, bound, split=(), dtype=jnp.bfloat16):
    values = jax.random.normal(stream_key, shape, jnp.float32) * spread
    if len(split) > 0:
        values = block_scale(stream_key, shape, split, -0.22, 0.18) * values
    return jnp.clip(values, min=-bound, max=bound).astype(dtype)


def setup_inputs(seed: int = 0) -> dict:
    arg_keys = jax.random.split(jax.random.key(seed), 8)
    inputs = scatter_about(arg_keys[0], (STEPS, IN, NH, NW), 1.0, 6.0, ((2, 16), (3, 16)))
    gate_pre = scatter_about(arg_keys[1], (STEPS, GATES, NH, NW), 1.5, 8.0, ((2, 16), (3, 16)))
    cotangent = scatter_about(arg_keys[2], (STEPS, HID, NH, NW), 1.0, 6.0, ((2, 16), (3, 16)))
    hidden_init = scatter_about(arg_keys[3], (HID, NH, NW), 1.0, 6.0, ((1, 16), (2, 16)))
    cell_init = scatter_about(arg_keys[4], (HID, NH, NW), 1.0, 6.0, ((1, 16), (2, 16)), jnp.float32)
    land_mask = place_ends((jax.random.randint(arg_keys[5], (NH, NW), 0, 4) < 3).astype(jnp.int32), jax.random.fold_in(arg_keys[5], 1), 0, 1)
    kernel = scatter_about(arg_keys[6], (GATES, TAPS), TAPS ** -0.5, 0.1875)
    return {"inputs": inputs, "gate_pre": gate_pre, "cotangent": cotangent, "hidden_init": hidden_init, "cell_init": cell_init, "land_mask": land_mask, "kernel": kernel}


def gate_parts(pre, hidden):
    return (jax.nn.sigmoid(pre[:hidden]), jax.nn.sigmoid(pre[hidden:2 * hidden]), jax.nn.sigmoid(pre[2 * hidden:3 * hidden]), jnp.tanh(pre[3 * hidden:]))

def kernel_terms(grads, padded, rows, cols):
    flat = grads.reshape(grads.shape[0], rows * cols)
    blocks = []
    for offset in range(9):
        upper, left = (offset // 3, offset % 3)
        window = padded[:, upper:upper + rows, left:left + cols].reshape(padded.shape[0], rows * cols)
        blocks.append(lax.dot_general(flat, window, (((1,), (1,)), ((), ())), preferred_element_type=jnp.float32))
    return jnp.concatenate(blocks, axis=1)

def transposed(kernel, padded_grads, rows, cols, width):
    total = jnp.zeros((width, rows * cols), jnp.float32)
    for offset in range(9):
        upper, left = (offset // 3, offset % 3)
        window = padded_grads[:, 2 - upper:2 - upper + rows, 2 - left:2 - left + cols]
        window = window.reshape(padded_grads.shape[0], rows * cols)
        piece = kernel[:, offset * width:(offset + 1) * width]
        total = total + lax.dot_general(piece, window, (((0,), (0,)), ((), ())), preferred_element_type=jnp.float32)
    return total

def reference(inputs, gate_pre, cotangent, hidden_init, cell_init, land_mask, kernel):
    mask = land_mask.astype(jnp.float32)
    scale = 1.0 / jnp.sqrt(jnp.float32(NH * NW))
    width = IN + HID
    states = [cell_init]
    layers = []
    hidden_now = hidden_init
    acts = []
    for step in range(STEPS):
        gates = gate_parts(gate_pre[step].astype(jnp.float32), HID)
        acts.append(gates)
        layers.append(jnp.concatenate([inputs[step], hidden_now], axis=0))
        new_cell = gates[1] * states[-1] + gates[0] * gates[3]
        states.append(new_cell)
        hidden_now = (mask * gates[2] * jnp.tanh(new_cell)).astype(jnp.bfloat16)
    grad_h = jnp.zeros((HID, NH, NW), jnp.float32)
    grad_c = jnp.zeros((HID, NH, NW), jnp.float32)
    kernel_total = jnp.zeros((4 * HID, 9 * width), jnp.float32)
    bias_total = jnp.zeros((4 * HID,), jnp.float32)
    outs = [None] * STEPS
    for step in reversed(range(STEPS)):
        gin, gfor, gout, gcand = acts[step]
        tanh_cell = jnp.tanh(states[step + 1])
        error = mask * (grad_h + cotangent[step].astype(jnp.float32))
        grad_c = grad_c + error * gout * (1.0 - tanh_cell * tanh_cell)
        grads = jnp.concatenate([grad_c * gcand * gin * (1.0 - gin), grad_c * states[step] * gfor * (1.0 - gfor), error * tanh_cell * gout * (1.0 - gout), grad_c * gin * (1.0 - gcand * gcand)], axis=0).astype(jnp.bfloat16)
        grad_c = grad_c * gfor
        padded = jnp.pad(layers[step], ((0, 0), (1, 1), (1, 1)))
        kernel_total = kernel_total + scale * kernel_terms(grads, padded, NH, NW)
        bias_total = bias_total + scale * lax.optimization_barrier(jnp.sum(grads.astype(jnp.float32), axis=(1, 2)))
        padded_grads = jnp.pad(grads, ((0, 0), (1, 1), (1, 1)))
        back = transposed(kernel, padded_grads, NH, NW, width)
        outs[step] = back[:IN].reshape(IN, NH, NW).astype(jnp.bfloat16)
        grad_h = back[IN:].reshape(HID, NH, NW)
    return (jnp.stack(outs), grad_h, grad_c, kernel_total, bias_total)
```

```python
import functools
import math

import jax
import jax.numpy as jnp
from jax import lax
from jax.experimental import pallas as pl
from jax.experimental.pallas import tpu as pltpu
from jax.sharding import PartitionSpec as P

INTERPRET = False
F32 = jnp.float32
BF16 = jnp.bfloat16
ROWS = 8
LANES = 128
SLABS = ROWS + 2
CH = 64
Q = 4 * CH
W = 2 * CH


def call(body, out_shape, in_specs=None, out_specs=None, scratch=(), aliases=None):
    kwargs = {}
    if in_specs is not None:
        kwargs["in_specs"] = in_specs
    if out_specs is not None:
        kwargs["out_specs"] = out_specs
    return pl.pallas_call(
        body,
        out_shape=out_shape,
        scratch_shapes=list(scratch),
        input_output_aliases=aliases or {},
        interpret=INTERPRET,
        grid=(1,),
        **kwargs,
    )


def whole():
    return pl.BlockSpec(memory_space=pltpu.VMEM)


def at_step(step, shape):
    return pl.BlockSpec((1,) + shape, lambda i: (step,) + (0,) * len(shape))


def sigmoid(x):
    return 0.5 * jnp.tanh(0.5 * x) + 0.5


def lane_ids(rows):
    return lax.broadcasted_iota(jnp.int32, (rows, LANES), 1)


def parity(axis):
    return lax.rem(lax.axis_index(axis), 2)


def edge_flags(axis):
    index = lax.axis_index(axis)
    low = jnp.where(index > 0, 1.0, 0.0).astype(F32)
    high = jnp.where(index < lax.axis_size(axis) - 1, 1.0, 0.0).astype(F32)
    return low, high


def gate_grads(pre, part, cot, dh, mask, cell_before, tanh_cell, dc):
    gin, gfor, gout, gcand = pre
    error = mask * (cot if dh is None else dh + cot)
    eo = error * gout
    grad = eo * (1.0 - tanh_cell * tanh_cell)
    if dc is not None:
        grad = dc + grad
    gi = grad * gin
    part[0] = gi * gcand * (1.0 - gin)
    df = grad * gfor
    part[1] = df * cell_before * (1.0 - gfor)
    part[2] = eo * tanh_cell * (1.0 - gout)
    part[3] = gi * (1.0 - gcand * gcand)
    return df


def emit_grads(scr, a_ref, p0_ref, p1_ref, ql_ref, qr_ref):
    par = parity("row")
    step = 32
    lanes = lane_ids(step)
    for k in range(Q // step):
        own = pl.ds(k * step, step)
        ql = jnp.zeros((step, LANES), F32)
        qr = jnp.zeros((step, LANES), F32)
        for r in range(ROWS):
            row = scr[pl.ds(k * step * ROWS + r, step, stride=ROWS), :]
            a_ref[own, r * LANES : (r + 1) * LANES] = row.astype(BF16)
            ql = jnp.where(lanes == r + 1, pltpu.roll(row, r + 1, 1), ql)
            qr = jnp.where(lanes == r + 1, pltpu.roll(row, r + 2, 1), qr)
        ql_ref[own, :] = ql.astype(BF16)
        qr_ref[own, :] = qr.astype(BF16)
    top = a_ref[:, 0:LANES]
    bottom = a_ref[:, (ROWS - 1) * LANES :]

    @pl.when(par == 0)
    def _():
        p0_ref[...] = bottom
        p1_ref[...] = top

    @pl.when(par == 1)
    def _():
        p0_ref[...] = top
        p1_ref[...] = bottom


def forward_kernel(pre_ref, cot_ref, h_ref_unused, c0_ref, mask_ref, c1_ref, c2_ref, h1_ref, h2_ref, dc_ref, a_ref, p0_ref, p1_ref, ql_ref, qr_ref, scr):
    del h_ref_unused
    step = 4
    mask = mask_ref[...].astype(F32)[None]

    def chunk(j, carry):
        base = j * step

        def gate(t, g):
            return pre_ref[t, pl.ds(g * CH + base, step)].astype(F32)

        own = pl.ds(base, step)
        cell = c0_ref[own]
        for t, (c_ref, h_ref) in enumerate(((c1_ref, h1_ref), (c2_ref, h2_ref))):
            cell = sigmoid(gate(t, 1)) * cell + sigmoid(gate(t, 0)) * jnp.tanh(gate(t, 3))
            c_ref[own] = cell
            h_ref[own] = (mask * sigmoid(gate(t, 2)) * jnp.tanh(cell)).astype(BF16)
        pre = (sigmoid(gate(2, 0)), sigmoid(gate(2, 1)), sigmoid(gate(2, 2)), jnp.tanh(gate(2, 3)))
        tanh_cell = jnp.tanh(pre[1] * cell + pre[0] * pre[3])
        part = [None] * 4
        dc_ref[own] = gate_grads(pre, part, cot_ref[0, own].astype(F32), None, mask, cell, tanh_cell, None)
        for g in range(4):
            scr[pl.ds((g * CH + base) * ROWS, step * ROWS), :] = part[g].reshape(step * ROWS, LANES)
        return carry

    lax.fori_loop(0, CH // step, chunk, 0)
    emit_grads(scr, a_ref, p0_ref, p1_ref, ql_ref, qr_ref)


def halo_rows(r0_ref, r1_ref, own):
    par = parity("row").astype(F32)
    low, high = edge_flags("row")
    first, second = r0_ref[own, :].astype(F32), r1_ref[own, :].astype(F32)
    above = second * ((1.0 - par) * low) + first * (par * low)
    below = first * ((1.0 - par) * high) + second * (par * high)
    return above, below


def corner_kernel(r0_ref, r1_ref, ql_ref, qr_ref, c0_ref, c1_ref):
    par = parity("col").astype(F32)
    step = 32
    lanes = lane_ids(step)
    for k in range(Q // step):
        own = pl.ds(k * step, step)
        above, below = halo_rows(r0_ref, r1_ref, own)
        left = jnp.where(lanes == 0, above, ql_ref[own, :].astype(F32))
        left = jnp.where(lanes == SLABS - 1, pltpu.roll(below, SLABS - 1, 1), left)
        right = jnp.where(lanes == 0, pltpu.roll(above, 1, 1), qr_ref[own, :].astype(F32))
        right = jnp.where(lanes == SLABS - 1, pltpu.roll(below, SLABS, 1), right)
        c0_ref[own, :] = (right * (1.0 - par) + left * par).astype(BF16)
        c1_ref[own, :] = (left * (1.0 - par) + right * par).astype(BF16)


def build_windows(a_ref, r0_ref, r1_ref, c0_ref, c1_ref, b_ref):
    par = parity("col").astype(F32)
    low, high = edge_flags("col")
    step = 32
    lanes = lane_ids(step)
    for k in range(Q // step):
        own = pl.ds(k * step, step)
        above, below = halo_rows(r0_ref, r1_ref, own)
        first, second = c0_ref[own, :].astype(F32), c1_ref[own, :].astype(F32)
        left = second * ((1.0 - par) * low) + first * (par * low)
        right = first * ((1.0 - par) * high) + second * (par * high)
        for s in range(SLABS):
            if s == 0:
                row = above
            elif s == SLABS - 1:
                row = below
            else:
                row = a_ref[own, (s - 1) * LANES : s * LANES].astype(F32)
            span = slice(s * LANES, (s + 1) * LANES)
            minus = jnp.where(lanes == LANES - 1, pltpu.roll(right, LANES - 1 - s, 1), pltpu.roll(row, LANES - 1, 1))
            plus = jnp.where(lanes == 0, pltpu.roll(left, (LANES - s) % LANES, 1), pltpu.roll(row, 1, 1))
            b_ref[pl.ds(k * step, step), span] = minus.astype(BF16)
            b_ref[pl.ds(Q + k * step, step), span] = row.astype(BF16)
            b_ref[pl.ds(2 * Q + k * step, step), span] = plus.astype(BF16)


def convolve(w_ref, b_ref, y3, scr):
    y3[...] = lax.dot_general(w_ref[...], b_ref[...], (((1,), (0,)), ((), ())), preferred_element_type=F32)
    for r in range(ROWS):
        total = y3[0:W, (r + 2) * LANES : (r + 3) * LANES]
        total = total + y3[W : 2 * W, (r + 1) * LANES : (r + 2) * LANES]
        total = total + y3[2 * W : 3 * W, r * LANES : (r + 1) * LANES]
        scr[pl.ds(r, W, stride=ROWS), :] = total


def backward_kernel(has_gi, *refs):
    if has_gi:
        refs = refs[1:]
    (a_in, r0_ref, r1_ref, k0_ref, k1_ref, w_ref, pre_ref, cot_ref, before_ref, cell_ref, mask_ref, dc_in,
     gi_ref, b_ref, dc_ref, a_ref, p0_ref, p1_ref, ql_ref, qr_ref, y3, yscr, scr) = refs
    build_windows(a_in, r0_ref, r1_ref, k0_ref, k1_ref, b_ref)
    convolve(w_ref, b_ref, y3, yscr)
    step = 4
    mask = mask_ref[...].astype(F32)[None]

    def chunk(j, carry):
        base = j * step
        own = pl.ds(base, step)

        def gate(g):
            return pre_ref[0, pl.ds(g * CH + base, step)].astype(F32)

        gi_ref[0, own] = yscr[pl.ds(base * ROWS, step * ROWS), :].reshape(step, ROWS, LANES).astype(BF16)
        dh = yscr[pl.ds((CH + base) * ROWS, step * ROWS), :].reshape(step, ROWS, LANES)
        pre = (sigmoid(gate(0)), sigmoid(gate(1)), sigmoid(gate(2)), jnp.tanh(gate(3)))
        part = [None] * 4
        dc_ref[own] = gate_grads(pre, part, cot_ref[0, own].astype(F32), dh, mask, before_ref[own], jnp.tanh(cell_ref[own]), dc_in[own])
        for g in range(4):
            scr[pl.ds((g * CH + base) * ROWS, step * ROWS), :] = part[g].reshape(step * ROWS, LANES)
        return carry

    lax.fori_loop(0, CH // step, chunk, 0)
    emit_grads(scr, a_ref, p0_ref, p1_ref, ql_ref, qr_ref)


def last_kernel(gi_in, a_in, r0_ref, r1_ref, k0_ref, k1_ref, w_ref, gi_ref, b_ref, dh_ref, y3, yscr):
    del gi_in
    build_windows(a_in, r0_ref, r1_ref, k0_ref, k1_ref, b_ref)
    convolve(w_ref, b_ref, y3, yscr)
    gi_ref[0] = yscr[0 : CH * ROWS, :].reshape(CH, ROWS, LANES).astype(BF16)
    dh_ref[...] = yscr[CH * ROWS :, :].reshape(CH, ROWS, LANES)


ZROWS = 3 * W + 16


def kernel_grads(x_ref, h_ref, b_ref, z3, tmp):
    tmp[0 : CH * ROWS, :] = x_ref[0].astype(F32).reshape(CH * ROWS, LANES)
    tmp[CH * ROWS :, :] = h_ref[...].astype(F32).reshape(CH * ROWS, LANES)
    zero = jnp.zeros((W, LANES), BF16)
    for u in range(3):
        for s in range(SLABS):
            if not 0 <= s - 2 + u < ROWS:
                z3[u * W : (u + 1) * W, s * LANES : (s + 1) * LANES] = zero
    for r in range(ROWS):
        row = tmp[pl.ds(r, W, stride=ROWS), :].astype(BF16)
        for u in range(3):
            s = r + 2 - u
            z3[u * W : (u + 1) * W, s * LANES : (s + 1) * LANES] = row
    row_id = lax.broadcasted_iota(jnp.int32, (16, SLABS * LANES), 0)
    lane_id = lax.broadcasted_iota(jnp.int32, (16, SLABS * LANES), 1)
    inside = (row_id == 0) & (lane_id >= LANES) & (lane_id < (SLABS - 1) * LANES)
    z3[3 * W :, :] = jnp.where(inside, 1.0, 0.0).astype(BF16)
    dims = (((1,), (1,)), ((), ()))
    for v in range(3):
        span = 3 * W + 16 if v == 1 else 3 * W
        got = lax.dot_general(z3[0:span, :], b_ref[v * Q : (v + 1) * Q, :], dims, preferred_element_type=F32)
        for u in range(3):
            yield u * 3 + v, got[u * W : (u + 1) * W]
        if v == 1:
            yield 9, got[3 * W :]


def accumulate_kernel(has_acc, *refs):
    if has_acc:
        acc_ref, x_ref, h_ref, b_ref, out_ref, z3, tmp = refs
    else:
        x_ref, h_ref, b_ref, out_ref, z3, tmp = refs
    for tap, got in kernel_grads(x_ref, h_ref, b_ref, z3, tmp):
        rows = slice(tap * W, tap * W + got.shape[0])
        out_ref[rows, :] = acc_ref[rows, :] + got if has_acc else got


def send_kernel(blocks, scale, acc_ref, x_ref, h_ref, b_ref, out_ref, z3, tmp, total):
    for tap, got in kernel_grads(x_ref, h_ref, b_ref, z3, tmp):
        rows = slice(tap * W, tap * W + got.shape[0])
        total[rows, :] = (acc_ref[rows, :] + got) * scale
    bias = total[9 * W : 9 * W + 8, :]
    high = jnp.broadcast_to(bias[0:1], (8, Q)).astype(BF16).astype(F32)
    low = jnp.broadcast_to(bias[0:1], (8, Q)) - high
    ids = lax.broadcasted_iota(jnp.int32, (8, Q), 0)
    tail = jnp.where(ids == 0, high, jnp.where(ids == 1, low, 0.0))
    size = 9 * W // blocks
    for c in range(blocks):
        body = jnp.concatenate([total[c * size : (c + 1) * size, :], tail], axis=0)
        out_ref[c * (size + 8) : (c + 1) * (size + 8), :] = body.astype(BF16)


def fold_kernel(blocks, in_ref, out_ref):
    size = in_ref.shape[0] // blocks
    total = in_ref[0:size, :].astype(F32)
    for c in range(1, blocks):
        total = total + in_ref[c * size : (c + 1) * size, :].astype(F32)
    out_ref[...] = total.T


def even_swap(count):
    return [(i, i ^ 1) for i in range(count)]


def odd_swap(count):
    return [(i, (i + 1) % count if i % 2 else (i - 1) % count) for i in range(count)]


def swaps(first, second, axis):
    count = lax.axis_size(axis)
    return lax.ppermute(first, axis, even_swap(count)), lax.ppermute(second, axis, odd_swap(count))


def struct(shape, dtype):
    return jax.ShapeDtypeStruct(shape, dtype)


def shards(inputs, gate_pre, cotangent, hidden_init, cell_init, land_mask, kernel):
    field = (CH, ROWS, LANES)
    nrow, ncol = lax.axis_size("row"), lax.axis_size("col")
    scale = 1.0 / math.sqrt(ROWS * LANES * nrow * ncol)
    weights = kernel.reshape(Q, 3, 3, W).transpose(1, 3, 2, 0).reshape(3 * W, 3 * Q)
    edge = struct((Q, LANES), BF16)
    grads_out = (struct((Q, ROWS * LANES), BF16), edge, edge, edge, edge)
    scr = pltpu.VMEM((Q * ROWS, LANES), F32)
    y3, yscr = pltpu.VMEM((3 * W, SLABS * LANES), F32), pltpu.VMEM((W * ROWS, LANES), F32)
    z3, tmp = pltpu.VMEM((ZROWS, SLABS * LANES), BF16), pltpu.VMEM((W * ROWS, LANES), F32)

    c1, c2, h1, h2, dc, a, p0, p1, ql, qr = call(
        forward_kernel,
        (struct(field, F32), struct(field, F32), struct(field, BF16), struct(field, BF16), struct(field, F32)) + grads_out,
        in_specs=[whole(), at_step(2, field), whole(), whole(), whole()],
        out_specs=[whole()] * 10,
        scratch=[scr],
    )(gate_pre, cotangent, hidden_init, cell_init, land_mask)

    cells = [cell_init, c1, c2]
    hiddens = [hidden_init, h1, h2]
    gi_shape = struct((3,) + field, BF16)
    windows = struct((3 * Q, SLABS * LANES), BF16)
    acc_shape = struct((9 * W + 16, Q), F32)
    gi = acc = None
    for t in (2, 1, 0):
        r0, r1 = swaps(p0, p1, "row")
        k0, k1 = call(corner_kernel, (edge, edge), in_specs=[whole()] * 4, out_specs=[whole()] * 2)(r0, r1, ql, qr)
        k0, k1 = swaps(k0, k1, "col")
        if t > 0:
            head = [] if gi is None else [gi]
            gi, b, dc, a_next, p0, p1, ql, qr = call(
                functools.partial(backward_kernel, gi is not None),
                (gi_shape, windows, struct(field, F32)) + grads_out,
                in_specs=[pl.BlockSpec(memory_space=pl.ANY)] * len(head)
                + [whole()] * 6
                + [at_step(t - 1, (Q, ROWS, LANES)), at_step(t - 1, field)]
                + [whole()] * 4,
                out_specs=[at_step(t, field)] + [whole()] * 7,
                scratch=[y3, yscr, scr],
                aliases={0: 0} if head else {},
            )(*head, a, r0, r1, k0, k1, weights, gate_pre, cotangent, cells[t - 1], cells[t], land_mask, dc)
            a = a_next
            head = [] if acc is None else [acc]
            acc = call(
                functools.partial(accumulate_kernel, acc is not None),
                acc_shape,
                in_specs=[whole()] * len(head) + [at_step(t, field), whole(), whole()],
                out_specs=whole(),
                scratch=[z3, tmp],
                aliases={0: 0} if head else {},
            )(*head, inputs, hiddens[t], b)
        else:
            gi, b, grad_hidden = call(
                last_kernel,
                (gi_shape, windows, struct(field, F32)),
                in_specs=[pl.BlockSpec(memory_space=pl.ANY)] + [whole()] * 6,
                out_specs=[at_step(0, field), whole(), whole()],
                scratch=[y3, yscr],
                aliases={0: 0},
            )(gi, a, r0, r1, k0, k1, weights)
            size = 9 * W // ncol + 8
            send = call(
                functools.partial(send_kernel, ncol, scale),
                struct((ncol * size, Q), BF16),
                in_specs=[whole(), at_step(0, field), whole(), whole()],
                out_specs=whole(),
                scratch=[z3, tmp, pltpu.VMEM((9 * W + 16, Q), F32)],
            )(acc, inputs, hiddens[0], b)
    got = lax.all_to_all(send, "col", 0, 0, tiled=True)
    folded = call(functools.partial(fold_kernel, ncol), struct((Q, size), F32), in_specs=[whole()], out_specs=whole())(got)
    got = lax.all_to_all(folded, "row", 0, 0, tiled=True)
    total = got.reshape(nrow, Q // nrow, size).sum(0)
    bias = total[:, size - 8] + total[:, size - 7]
    count = Q // nrow // ncol
    grad_bias = lax.dynamic_slice_in_dim(bias, lax.axis_index("col") * count, count)
    return (gi, grad_hidden, dc, total[:, : size - 8], grad_bias)


def solution(mesh):
    placed = (
        P(None, None, "row", "col"),
        P(None, None, "row", "col"),
        P(None, None, "row", "col"),
        P(None, "row", "col"),
        P(None, "row", "col"),
        P("row", "col"),
        P(),
    )
    return jax.shard_map(
        shards,
        mesh=mesh,
        in_specs=placed,
        out_specs=(
            P(None, None, "row", "col"),
            P(None, "row", "col"),
            P(None, "row", "col"),
            P("row", "col"),
            P(("row", "col")),
        ),
        check_vma=False,
    )
```

```python
import functools
import math

import jax
import jax.numpy as jnp
from jax import lax
from jax.experimental import pallas as pl
from jax.experimental.pallas import tpu as pltpu
from jax.sharding import PartitionSpec as P

INTERPRET = False
VMEM_LIMIT = 24 << 20
F32 = jnp.float32
BF16 = jnp.bfloat16
ROWS = 8
LANES = 128
SLABS = ROWS + 2
CH = 64
Q = 4 * CH
W = 2 * CH


def call(body, out_shape, in_specs=None, out_specs=None, scratch=(), aliases=None):
    kwargs = {}
    if in_specs is not None:
        kwargs["in_specs"] = in_specs
    if out_specs is not None:
        kwargs["out_specs"] = out_specs
    return pl.pallas_call(
        body,
        out_shape=out_shape,
        scratch_shapes=list(scratch),
        input_output_aliases=aliases or {},
        interpret=INTERPRET,
        grid=(1,),
        compiler_params=pltpu.CompilerParams(vmem_limit_bytes=VMEM_LIMIT),
        **kwargs,
    )


def whole():
    return pl.BlockSpec(memory_space=pltpu.VMEM)


def at_step(step, shape):
    return pl.BlockSpec((1,) + shape, lambda i: (step,) + (0,) * len(shape))


def in_hbm(x):
    return x if INTERPRET else pltpu.with_memory_space_constraint(x, pltpu.MemorySpace.HBM)


def sigmoid(x):
    return 0.5 * jnp.tanh(0.5 * x) + 0.5


def lane_ids(rows):
    return lax.broadcasted_iota(jnp.int32, (rows, LANES), 1)


def parity(axis):
    return lax.rem(lax.axis_index(axis), 2)


def edge_flags(axis):
    index = lax.axis_index(axis)
    low = jnp.where(index > 0, 1.0, 0.0).astype(F32)
    high = jnp.where(index < lax.axis_size(axis) - 1, 1.0, 0.0).astype(F32)
    return low, high


def gate_grads(pre, part, cot, dh, mask, cell_before, tanh_cell, dc):
    gin, gfor, gout, gcand = pre
    error = mask * (cot if dh is None else dh + cot)
    eo = error * gout
    grad = eo * (1.0 - tanh_cell * tanh_cell)
    if dc is not None:
        grad = dc + grad
    gi = grad * gin
    part[0] = gi * gcand * (1.0 - gin)
    df = grad * gfor
    part[1] = df * cell_before * (1.0 - gfor)
    part[2] = eo * tanh_cell * (1.0 - gout)
    part[3] = gi * (1.0 - gcand * gcand)
    return df


def emit_grads(scr, a_ref, p0_ref, p1_ref, ql_ref, qr_ref):
    par = parity("row")
    step = 32
    lanes = lane_ids(step)
    for k in range(Q // step):
        own = pl.ds(k * step, step)
        ql = jnp.zeros((step, LANES), F32)
        qr = jnp.zeros((step, LANES), F32)
        for r in range(ROWS):
            row = scr[pl.ds(k * step * ROWS + r, step, stride=ROWS), :]
            a_ref[own, r * LANES : (r + 1) * LANES] = row.astype(BF16)
            ql = jnp.where(lanes == r + 1, pltpu.roll(row, r + 1, 1), ql)
            qr = jnp.where(lanes == r + 1, pltpu.roll(row, r + 2, 1), qr)
        ql_ref[own, :] = ql.astype(BF16)
        qr_ref[own, :] = qr.astype(BF16)
    top = a_ref[:, 0:LANES]
    bottom = a_ref[:, (ROWS - 1) * LANES :]

    @pl.when(par == 0)
    def _():
        p0_ref[...] = bottom
        p1_ref[...] = top

    @pl.when(par == 1)
    def _():
        p0_ref[...] = top
        p1_ref[...] = bottom


def forward_kernel(pre_hbm, cot_hbm, c0_hbm, mask_hbm, c1_ref, c2_ref, h1_ref, h2_ref, dc_ref, a_ref, p0_ref, p1_ref, ql_ref, qr_ref, scr, pre_ref, cot_ref, c0_ref, mask_ref, sems):
    copies = [
        pltpu.make_async_copy(src, dst, sems.at[n])
        for n, (src, dst) in enumerate(
            [(c0_hbm, c0_ref), (mask_hbm, mask_ref)]
            + [(pre_hbm.at[t], pre_ref.at[t]) for t in range(3)]
            + [(cot_hbm.at[2], cot_ref)]
        )
    ]
    for copy in (copies[2], copies[0], copies[1], copies[3], copies[4], copies[5]):
        copy.start()
    step = 4

    def gate(t, g, base):
        return pre_ref[t, pl.ds(g * CH + base, step)].astype(F32)

    copies[0].wait()
    copies[1].wait()
    mask = mask_ref[...].astype(F32)[None]
    for t, (before_ref, c_ref, h_ref) in enumerate(((c0_ref, c1_ref, h1_ref), (c1_ref, c2_ref, h2_ref))):
        copies[2 + t].wait()

        def advance(j, carry):
            base = j * step
            own = pl.ds(base, step)
            cell = sigmoid(gate(t, 1, base)) * before_ref[own] + sigmoid(gate(t, 0, base)) * jnp.tanh(gate(t, 3, base))
            c_ref[own] = cell
            h_ref[own] = (mask * sigmoid(gate(t, 2, base)) * jnp.tanh(cell)).astype(BF16)
            return carry

        lax.fori_loop(0, CH // step, advance, 0)
    copies[4].wait()
    copies[5].wait()

    def chunk(j, carry):
        base = j * step
        own = pl.ds(base, step)
        cell = c2_ref[own]
        pre = (sigmoid(gate(2, 0, base)), sigmoid(gate(2, 1, base)), sigmoid(gate(2, 2, base)), jnp.tanh(gate(2, 3, base)))
        tanh_cell = jnp.tanh(pre[1] * cell + pre[0] * pre[3])
        part = [None] * 4
        dc_ref[own] = gate_grads(pre, part, cot_ref[own].astype(F32), None, mask, cell, tanh_cell, None)
        for g in range(4):
            scr[pl.ds((g * CH + base) * ROWS, step * ROWS), :] = part[g].reshape(step * ROWS, LANES)
        return carry

    lax.fori_loop(0, CH // step, chunk, 0)
    emit_grads(scr, a_ref, p0_ref, p1_ref, ql_ref, qr_ref)


def weights_kernel(k_ref, w_ref):
    for u in range(3):
        for v in range(3):
            tap = (3 * u + v) * W
            w_ref[u * W : (u + 1) * W, v * Q : (v + 1) * Q] = k_ref[:, tap : tap + W].astype(F32).T.astype(BF16)


def halo_rows(r0_ref, r1_ref, own):
    par = parity("row").astype(F32)
    low, high = edge_flags("row")
    first, second = r0_ref[own, :].astype(F32), r1_ref[own, :].astype(F32)
    above = second * ((1.0 - par) * low) + first * (par * low)
    below = first * ((1.0 - par) * high) + second * (par * high)
    return above, below


def corner_kernel(r0_ref, r1_ref, ql_ref, qr_ref, c0_ref, c1_ref):
    par = parity("col").astype(F32)
    step = 32
    lanes = lane_ids(step)
    for k in range(Q // step):
        own = pl.ds(k * step, step)
        above, below = halo_rows(r0_ref, r1_ref, own)
        left = jnp.where(lanes == 0, above, ql_ref[own, :].astype(F32))
        left = jnp.where(lanes == SLABS - 1, pltpu.roll(below, SLABS - 1, 1), left)
        right = jnp.where(lanes == 0, pltpu.roll(above, 1, 1), qr_ref[own, :].astype(F32))
        right = jnp.where(lanes == SLABS - 1, pltpu.roll(below, SLABS, 1), right)
        c0_ref[own, :] = (right * (1.0 - par) + left * par).astype(BF16)
        c1_ref[own, :] = (left * (1.0 - par) + right * par).astype(BF16)


def interior_kernel(a_ref, w_ref, b_ref, y_ref, y3):
    step = 32
    lanes = lane_ids(step)
    for k in range(Q // step):
        for r in range(ROWS):
            span = slice(r * LANES, (r + 1) * LANES)
            block = a_ref[pl.ds(k * step, step), span]
            row = block.astype(F32)
            minus = jnp.where(lanes == LANES - 1, 0.0, pltpu.roll(row, LANES - 1, 1))
            plus = jnp.where(lanes == 0, 0.0, pltpu.roll(row, 1, 1))
            b_ref[pl.ds(k * step, step), span] = minus.astype(BF16)
            b_ref[pl.ds(Q + k * step, step), span] = block
            b_ref[pl.ds(2 * Q + k * step, step), span] = plus.astype(BF16)
    y3[...] = lax.dot_general(w_ref[...], b_ref[...], (((1,), (0,)), ((), ())), preferred_element_type=F32)
    for r in range(ROWS):
        total = y3[W : 2 * W, r * LANES : (r + 1) * LANES]
        if r < ROWS - 1:
            total = total + y3[0:W, (r + 1) * LANES : (r + 2) * LANES]
        if r > 0:
            total = total + y3[2 * W : 3 * W, (r - 1) * LANES : r * LANES]
        y_ref[:, r * LANES : (r + 1) * LANES] = total


def build_halo(r0_ref, r1_ref, c0_ref, c1_ref, b_ref):
    par = parity("col").astype(F32)
    low, high = edge_flags("col")
    step = 32
    lanes = lane_ids(step)
    inside = (lanes >= 1) & (lanes <= ROWS)
    last = SLABS - 1
    for k in range(Q // step):
        own = pl.ds(k * step, step)
        above, below = halo_rows(r0_ref, r1_ref, own)
        first, second = c0_ref[own, :].astype(F32), c1_ref[own, :].astype(F32)
        left = second * ((1.0 - par) * low) + first * (par * low)
        right = first * ((1.0 - par) * high) + second * (par * high)
        for n, (row, s) in enumerate(((above, 0), (below, last))):
            span = slice(n * LANES, (n + 1) * LANES)
            minus = jnp.where(lanes == LANES - 1, pltpu.roll(right, LANES - 1 - s, 1), pltpu.roll(row, LANES - 1, 1))
            plus = jnp.where(lanes == 0, pltpu.roll(left, (LANES - s) % LANES, 1), pltpu.roll(row, 1, 1))
            b_ref[pl.ds(k * step, step), span] = minus.astype(BF16)
            b_ref[pl.ds(Q + k * step, step), span] = row.astype(BF16)
            b_ref[pl.ds(2 * Q + k * step, step), span] = plus.astype(BF16)
        span = slice(2 * LANES, 3 * LANES)
        b_ref[pl.ds(k * step, step), span] = jnp.where(inside, right, 0.0).astype(BF16)
        b_ref[pl.ds(Q + k * step, step), span] = jnp.zeros((step, LANES), BF16)
        b_ref[pl.ds(2 * Q + k * step, step), span] = pltpu.roll(jnp.where(inside, left, 0.0), LANES // 2, 1).astype(BF16)


def finish_y(w_ref, b_ref, y_ref, y3, scr):
    y3[...] = lax.dot_general(w_ref[...], b_ref[...], (((1,), (0,)), ((), ())), preferred_element_type=F32)
    step = 32
    lanes = lane_ids(step)
    for k in range(W // step):
        side = 0.0
        for u in range(3):
            piece = y3[pl.ds(u * W + k * step, step), 2 * LANES :]
            side = side + (piece if u == 2 else pltpu.roll(piece, LANES + u - 2, 1))
        for r in range(ROWS):
            total = y_ref[pl.ds(k * step, step), r * LANES : (r + 1) * LANES]
            if r == 0:
                total = total + y3[pl.ds(2 * W + k * step, step), 0:LANES]
            if r == ROWS - 1:
                total = total + y3[pl.ds(k * step, step), LANES : 2 * LANES]
            right = jnp.where(lanes == LANES - 1, pltpu.roll(side, LANES - 1 - r, 1), 0.0)
            left = jnp.where(lanes == 0, pltpu.roll(side, LANES // 2 - r, 1), right)
            scr[pl.ds(k * step * ROWS + r, step, stride=ROWS), :] = total + left


def backward_kernel(has_gi, *refs):
    if has_gi:
        refs = refs[1:]
    (r0_ref, r1_ref, k0_ref, k1_ref, w_ref, y_ref, pre_ref, cot_ref, before_ref, cell_ref, mask_ref, dc_in,
     gi_ref, b_ref, dc_ref, a_ref, p0_ref, p1_ref, ql_ref, qr_ref, y3, yscr, scr) = refs
    build_halo(r0_ref, r1_ref, k0_ref, k1_ref, b_ref)
    finish_y(w_ref, b_ref, y_ref, y3, yscr)
    step = 4
    mask = mask_ref[...].astype(F32)[None]

    def chunk(j, carry):
        base = j * step
        own = pl.ds(base, step)

        def gate(g):
            return pre_ref[0, pl.ds(g * CH + base, step)].astype(F32)

        gi_ref[0, own] = yscr[pl.ds(base * ROWS, step * ROWS), :].reshape(step, ROWS, LANES).astype(BF16)
        dh = yscr[pl.ds((CH + base) * ROWS, step * ROWS), :].reshape(step, ROWS, LANES)
        pre = (sigmoid(gate(0)), sigmoid(gate(1)), sigmoid(gate(2)), jnp.tanh(gate(3)))
        part = [None] * 4
        dc_ref[own] = gate_grads(pre, part, cot_ref[0, own].astype(F32), dh, mask, before_ref[own], jnp.tanh(cell_ref[own]), dc_in[own])
        for g in range(4):
            scr[pl.ds((g * CH + base) * ROWS, step * ROWS), :] = part[g].reshape(step * ROWS, LANES)
        return carry

    lax.fori_loop(0, CH // step, chunk, 0)
    emit_grads(scr, a_ref, p0_ref, p1_ref, ql_ref, qr_ref)


def last_kernel(gi_in, w_ref, y_ref, b_ref, gi_ref, dh_ref, y3, yscr):
    del gi_in
    finish_y(w_ref, b_ref, y_ref, y3, yscr)
    gi_ref[0] = yscr[0 : CH * ROWS, :].reshape(CH, ROWS, LANES).astype(BF16)
    dh_ref[...] = yscr[CH * ROWS :, :].reshape(CH, ROWS, LANES)


ZROWS = 3 * W + 16
CELLS = ROWS * LANES
CONTRACT_LANES = (((1,), (1,)), ((), ()))


def stack_fields(x_ref, h_ref, tmp):
    tmp[0 : CH * ROWS, :] = x_ref[0].astype(F32).reshape(CH * ROWS, LANES)
    tmp[CH * ROWS :, :] = h_ref[...].astype(F32).reshape(CH * ROWS, LANES)


def taps(z3, b_ref, bias):
    for v in range(3):
        span = ZROWS if bias and v == 1 else 3 * W
        got = lax.dot_general(z3[0:span, :], b_ref[v * Q : (v + 1) * Q, :], CONTRACT_LANES, preferred_element_type=F32)
        for u in range(3):
            yield u * 3 + v, got[u * W : (u + 1) * W]
        if bias and v == 1:
            yield 9, got[3 * W :]


def interior_taps(tmp, b_ref, z3):
    zero = jnp.zeros((W, LANES), BF16)
    z3[0:W, 0:LANES] = zero
    z3[2 * W : 3 * W, CELLS - LANES :] = zero
    for r in range(ROWS):
        row = tmp[pl.ds(r, W, stride=ROWS), :].astype(BF16)
        for u in range(3):
            n = r + 1 - u
            if 0 <= n < ROWS:
                z3[u * W : (u + 1) * W, n * LANES : (n + 1) * LANES] = row
    ids = lax.broadcasted_iota(jnp.int32, (16, CELLS), 0)
    z3[3 * W :, :] = jnp.where(ids == 0, 1.0, 0.0).astype(BF16)
    yield from taps(z3, b_ref, True)


def halo_taps(tmp, b_ref, zh):
    zero = jnp.zeros((W, LANES), BF16)
    zh[0:W, 0:LANES] = zero
    zh[W : 2 * W, 0:LANES] = zero
    zh[2 * W :, 0:LANES] = tmp[pl.ds(0, W, stride=ROWS), :].astype(BF16)
    zh[0:W, LANES : 2 * LANES] = tmp[pl.ds(ROWS - 1, W, stride=ROWS), :].astype(BF16)
    zh[W : 2 * W, LANES : 2 * LANES] = zero
    zh[2 * W :, LANES : 2 * LANES] = zero
    step = 32
    lanes = lane_ids(step)
    half = LANES // 2
    for k in range(W // step):
        side = jnp.zeros((step, LANES), F32)
        for r in range(ROWS):
            row = tmp[pl.ds(k * step * ROWS + r, step, stride=ROWS), :]
            side = jnp.where(lanes == r, pltpu.roll(row, r + 1, 1), side)
            side = jnp.where(lanes == half + r, pltpu.roll(row, half + r, 1), side)
        for u in range(3):
            zh[pl.ds(u * W + k * step, step), 2 * LANES :] = (side if u == 2 else pltpu.roll(side, 2 - u, 1)).astype(BF16)
    yield from taps(zh, b_ref, False)


def accumulate_kernel(has_acc, with_halo, *refs):
    refs = list(refs)
    acc_ref = refs.pop(0) if has_acc else None
    x_ref, h_ref, b_ref = refs[:3]
    out_ref, z3, zh, tmp = refs[-4:]
    stack_fields(x_ref, h_ref, tmp)
    for tap, got in interior_taps(tmp, b_ref, z3):
        rows = slice(tap * W, tap * W + got.shape[0])
        out_ref[rows, :] = acc_ref[rows, :] + got if has_acc else got
    if with_halo:
        for tap, got in halo_taps(tmp, refs[3], zh):
            rows = slice(tap * W, tap * W + got.shape[0])
            out_ref[rows, :] += got


def send_kernel(blocks, scale, acc_ref, x_ref, h_ref, r0_ref, r1_ref, k0_ref, k1_ref, out_ref, b_ref, zh, tmp, total):
    build_halo(r0_ref, r1_ref, k0_ref, k1_ref, b_ref)
    stack_fields(x_ref, h_ref, tmp)
    for tap, got in halo_taps(tmp, b_ref, zh):
        rows = slice(tap * W, tap * W + got.shape[0])
        total[rows, :] = (acc_ref[rows, :] + got) * scale
    bias = acc_ref[9 * W : 9 * W + 8, :] * scale
    high = jnp.broadcast_to(bias[0:1], (8, Q)).astype(BF16).astype(F32)
    low = jnp.broadcast_to(bias[0:1], (8, Q)) - high
    ids = lax.broadcasted_iota(jnp.int32, (8, Q), 0)
    tail = jnp.where(ids == 0, high, jnp.where(ids == 1, low, 0.0))
    size = 9 * W // blocks
    for c in range(blocks):
        body = jnp.concatenate([total[c * size : (c + 1) * size, :], tail], axis=0)
        out_ref[c * (size + 8) : (c + 1) * (size + 8), :] = body.astype(BF16)


def result_kernel(blocks, in_ref, k_ref, bias_ref, scr):
    size = in_ref.shape[0] // blocks
    total = in_ref[0:size, :]
    for c in range(1, blocks):
        total = total + in_ref[c * size : (c + 1) * size, :]
    taps_here = k_ref.shape[1]
    k_ref[...] = total[:, 0:taps_here]
    scr[...] = jnp.broadcast_to(total[:, taps_here : taps_here + 1] + total[:, taps_here + 1 : taps_here + 2], scr.shape)
    count = bias_ref.shape[0]
    bias_ref[...] = scr[pl.ds(lax.axis_index("col") * count, count), 0:1]


def fold_kernel(blocks, in_ref, out_ref):
    size = in_ref.shape[0] // blocks
    total = in_ref[0:size, :].astype(F32)
    for c in range(1, blocks):
        total = total + in_ref[c * size : (c + 1) * size, :].astype(F32)
    out_ref[...] = total.T


def even_swap(count):
    return [(i, i ^ 1) for i in range(count)]


def odd_swap(count):
    return [(i, (i + 1) % count if i % 2 else (i - 1) % count) for i in range(count)]


def swaps(first, second, axis):
    count = lax.axis_size(axis)
    return lax.ppermute(first, axis, even_swap(count)), lax.ppermute(second, axis, odd_swap(count))


def struct(shape, dtype):
    return jax.ShapeDtypeStruct(shape, dtype)


def shards(inputs, gate_pre, cotangent, hidden_init, cell_init, land_mask, kernel):
    field = (CH, ROWS, LANES)
    nrow, ncol = lax.axis_size("row"), lax.axis_size("col")
    scale = 1.0 / math.sqrt(ROWS * LANES * nrow * ncol)
    edge = struct((Q, LANES), BF16)
    grads_out = (struct((Q, CELLS), BF16), edge, edge, edge, edge)
    scr = pltpu.VMEM((Q * ROWS, LANES), F32)
    y3 = pltpu.VMEM((3 * W, 3 * LANES), F32)
    tmp = pltpu.VMEM((W * ROWS, LANES), F32)
    z3, zh = pltpu.VMEM((ZROWS, CELLS), BF16), pltpu.VMEM((3 * W, 3 * LANES), BF16)
    hbm = pl.BlockSpec(memory_space=pltpu.MemorySpace.HBM)

    c1, c2, h1, h2, dc, a, p0, p1, ql, qr = call(
        forward_kernel,
        (struct(field, F32), struct(field, F32), struct(field, BF16), struct(field, BF16), struct(field, F32)) + grads_out,
        in_specs=[hbm] * 4,
        out_specs=[whole()] * 10,
        scratch=[
            scr,
            pltpu.VMEM((3, Q, ROWS, LANES), BF16),
            pltpu.VMEM(field, BF16),
            pltpu.VMEM(field, F32),
            pltpu.VMEM((ROWS, LANES), jnp.int32),
            pltpu.SemaphoreType.DMA((6,)),
        ],
    )(*(in_hbm(x) for x in (gate_pre, cotangent, cell_init, land_mask)))

    cells = [cell_init, c1, c2]
    hiddens = [hidden_init, h1, h2]
    gi_shape = struct((3,) + field, BF16)
    interior, halo = struct((3 * Q, CELLS), BF16), struct((3 * Q, 3 * LANES), BF16)
    acc_shape = struct((ZROWS + 6 * W, Q), F32)

    def accumulate(t, acc, b, bh):
        head = [] if acc is None else [acc]
        rest = [b] if bh is None else [b, bh]
        return call(
            functools.partial(accumulate_kernel, acc is not None, bh is not None),
            acc_shape,
            in_specs=[whole()] * len(head) + [at_step(t, field)] + [whole()] * (1 + len(rest)),
            out_specs=whole(),
            scratch=[z3, zh, tmp],
            aliases={0: 0} if head else {},
        )(*head, inputs, hiddens[t], *rest)

    gi = acc = weights = b = bh = None
    for t in (2, 1, 0):
        r0, r1 = swaps(p0, p1, "row")
        if t == 2:
            weights = call(weights_kernel, struct((3 * W, 3 * Q), BF16), in_specs=[whole()], out_specs=whole())(kernel)
            r0, r1, weights = lax.optimization_barrier((r0, r1, weights))
        else:
            acc = accumulate(t + 1, acc, b, bh)
            r0, r1, acc = lax.optimization_barrier((r0, r1, acc))
        k0, k1 = call(corner_kernel, (edge, edge), in_specs=[whole()] * 4, out_specs=[whole()] * 2)(r0, r1, ql, qr)
        k0, k1 = swaps(k0, k1, "col")
        b, y = call(
            interior_kernel,
            (interior, struct((W, CELLS), F32)),
            in_specs=[whole()] * 2,
            out_specs=[whole()] * 2,
            scratch=[pltpu.VMEM((3 * W, CELLS), F32)],
        )(a, weights)
        if t > 0:
            head = [] if gi is None else [gi]
            gi, bh, dc, a, p0, p1, ql, qr = call(
                functools.partial(backward_kernel, gi is not None),
                (gi_shape, halo, struct(field, F32)) + grads_out,
                in_specs=[pl.BlockSpec(memory_space=pl.ANY)] * len(head)
                + [whole()] * 6
                + [at_step(t - 1, (Q, ROWS, LANES)), at_step(t - 1, field)]
                + [whole()] * 4,
                out_specs=[at_step(t, field)] + [whole()] * 7,
                scratch=[y3, tmp, scr],
                aliases={0: 0} if head else {},
            )(*head, r0, r1, k0, k1, weights, y, gate_pre, cotangent, cells[t - 1], cells[t], land_mask, dc)
    acc = accumulate(0, acc, b, None)
    size = 9 * W // ncol + 8
    send, bh = call(
        functools.partial(send_kernel, ncol, scale),
        (struct((ncol * size, Q), BF16), halo),
        in_specs=[whole(), at_step(0, field)] + [whole()] * 5,
        out_specs=[whole()] * 2,
        scratch=[zh, tmp, pltpu.VMEM((9 * W, Q), F32)],
    )(acc, inputs, hiddens[0], r0, r1, k0, k1)
    got = lax.all_to_all(send, "col", 0, 0, tiled=True)
    folded = call(functools.partial(fold_kernel, ncol), struct((Q, size), F32), in_specs=[whole()], out_specs=whole())(got)
    got = lax.all_to_all(folded, "row", 0, 0, tiled=True)
    y, folded = lax.optimization_barrier((y, folded))
    gi, grad_hidden = call(
        last_kernel,
        (gi_shape, struct(field, F32)),
        in_specs=[pl.BlockSpec(memory_space=pl.ANY)] + [whole()] * 3,
        out_specs=[at_step(0, field), whole()],
        scratch=[y3, tmp],
        aliases={0: 0},
    )(gi, weights, y, bh)
    count = Q // nrow // ncol
    grad_kernel, grad_bias = call(
        functools.partial(result_kernel, nrow),
        (struct((Q // nrow, size - 8), F32), struct((count, 1), F32)),
        in_specs=[whole()],
        out_specs=[whole()] * 2,
        scratch=[pltpu.VMEM((Q // nrow, LANES), F32)],
    )(got)
    return (gi, grad_hidden, dc, grad_kernel, grad_bias.reshape(count))


def solution(mesh):
    placed = (
        P(None, None, "row", "col"),
        P(None, None, "row", "col"),
        P(None, None, "row", "col"),
        P(None, "row", "col"),
        P(None, "row", "col"),
        P("row", "col"),
        P(),
    )
    return jax.shard_map(
        shards,
        mesh=mesh,
        in_specs=placed,
        out_specs=(
            P(None, None, "row", "col"),
            P(None, "row", "col"),
            P(None, "row", "col"),
            P("row", "col"),
            P(("row", "col")),
        ),
        check_vma=False,
    )
```

```python
import functools
import math

import jax
import jax.numpy as jnp
from jax import lax
from jax.experimental import pallas as pl
from jax.experimental.pallas import tpu as pltpu
from jax.sharding import PartitionSpec as P

INTERPRET = False
VMEM_LIMIT = 24 << 20
F32 = jnp.float32
BF16 = jnp.bfloat16
ROWS = 8
LANES = 128
SLABS = ROWS + 2
CH = 64
Q = 4 * CH
W = 2 * CH


def call(body, out_shape, in_specs=None, out_specs=None, scratch=(), aliases=None):
    kwargs = {}
    if in_specs is not None:
        kwargs["in_specs"] = in_specs
    if out_specs is not None:
        kwargs["out_specs"] = out_specs
    return pl.pallas_call(
        body,
        out_shape=out_shape,
        scratch_shapes=list(scratch),
        input_output_aliases=aliases or {},
        interpret=INTERPRET,
        grid=(1,),
        compiler_params=pltpu.CompilerParams(vmem_limit_bytes=VMEM_LIMIT),
        **kwargs,
    )


def whole():
    return pl.BlockSpec(memory_space=pltpu.VMEM)


def in_hbm(x):
    return x if INTERPRET else pltpu.with_memory_space_constraint(x, pltpu.MemorySpace.HBM)


def sigmoid(x):
    return 0.5 * jnp.tanh(0.5 * x) + 0.5


def lane_ids(rows):
    return lax.broadcasted_iota(jnp.int32, (rows, LANES), 1)


def parity(axis):
    return lax.rem(lax.axis_index(axis), 2)


def edge_flags(axis):
    index = lax.axis_index(axis)
    low = jnp.where(index > 0, 1.0, 0.0).astype(F32)
    high = jnp.where(index < lax.axis_size(axis) - 1, 1.0, 0.0).astype(F32)
    return low, high


def gate_grads(pre, part, cot, dh, mask, cell_before, tanh_cell, dc):
    gin, gfor, gout, gcand = pre
    error = mask * (cot if dh is None else dh + cot)
    eo = error * gout
    grad = eo * (1.0 - tanh_cell * tanh_cell)
    if dc is not None:
        grad = dc + grad
    gi = grad * gin
    part[0] = gi * gcand * (1.0 - gin)
    df = grad * gfor
    part[1] = df * cell_before * (1.0 - gfor)
    part[2] = eo * tanh_cell * (1.0 - gout)
    part[3] = gi * (1.0 - gcand * gcand)
    return df


def by_parity(par, top, bottom, p0_ref, p1_ref, start):
    rows = slice(start, start + top.shape[0])

    @pl.when(par == 0)
    def _():
        p0_ref[rows, :] = bottom
        p1_ref[rows, :] = top

    @pl.when(par == 1)
    def _():
        p0_ref[rows, :] = top
        p1_ref[rows, :] = bottom


def emit_grads(scr, a_ref, p0_ref, p1_ref, ql_ref, qr_ref):
    par = parity("row")
    step = 32
    lanes = lane_ids(step)
    for k in range(Q // step):
        own = pl.ds(k * step, step)
        ql = jnp.zeros((step, LANES), F32)
        qr = jnp.zeros((step, LANES), F32)
        for r in range(ROWS):
            row = scr[pl.ds(k * step * ROWS + r, step, stride=ROWS), :]
            a_ref[own, r * LANES : (r + 1) * LANES] = row.astype(BF16)
            ql = jnp.where(lanes == r + 1, pltpu.roll(row, r + 1, 1), ql)
            qr = jnp.where(lanes == r + 1, pltpu.roll(row, r + 2, 1), qr)
        ql_ref[own, :] = ql.astype(BF16)
        qr_ref[own, :] = qr.astype(BF16)
    top = a_ref[:, 0:LANES]
    bottom = a_ref[:, (ROWS - 1) * LANES :]

    by_parity(par, top, bottom, p0_ref, p1_ref, 0)


def forward_kernel(pre_hbm, cot_hbm, c0_hbm, mask_hbm, c1_ref, c2_ref, dc_ref, a_ref, p0_ref, p1_ref, ql_ref, qr_ref, scr, pre_ref, cot_ref, c0_ref, mask_ref, sems):
    pairs = [(c0_hbm, c0_ref), (mask_hbm, mask_ref), (cot_hbm.at[2], cot_ref)]
    for t, g in ((0, 1), (0, 0), (0, 3), (1, 1), (1, 0), (1, 3), (2, 1), (2, 0), (2, 3), (2, 2)):
        own = pl.ds(g * CH, CH)
        pairs.append((pre_hbm.at[t, own], pre_ref.at[t, own]))
    copies = [pltpu.make_async_copy(src, dst, sems.at[n]) for n, (src, dst) in enumerate(pairs)]
    order = [3, 4, 0, 5, 6, 7, 8, 9, 10, 11, 12, 2, 1]
    for n in order:
        copies[n].start()
    step = 4

    def gate(t, g, base):
        return pre_ref[t, pl.ds(g * CH + base, step)].astype(F32)

    copies[0].wait()
    for t, (before_ref, c_ref) in enumerate(((c0_ref, c1_ref), (c1_ref, c2_ref))):
        for n in range(3 + 3 * t, 6 + 3 * t):
            copies[n].wait()

        def advance(j, carry):
            base = j * step
            own = pl.ds(base, step)
            c_ref[own] = sigmoid(gate(t, 1, base)) * before_ref[own] + sigmoid(gate(t, 0, base)) * jnp.tanh(gate(t, 3, base))
            return carry

        lax.fori_loop(0, CH // step, advance, 0)
    for n in (9, 10, 11, 12, 2, 1):
        copies[n].wait()
    mask = mask_ref[...].astype(F32)[None]

    def chunk(j, carry):
        base = j * step
        own = pl.ds(base, step)
        cell = c2_ref[own]
        pre = (sigmoid(gate(2, 0, base)), sigmoid(gate(2, 1, base)), sigmoid(gate(2, 2, base)), jnp.tanh(gate(2, 3, base)))
        tanh_cell = jnp.tanh(pre[1] * cell + pre[0] * pre[3])
        part = [None] * 4
        dc_ref[own] = gate_grads(pre, part, cot_ref[own].astype(F32), None, mask, cell, tanh_cell, None)
        for g in range(4):
            scr[pl.ds((g * CH + base) * ROWS, step * ROWS), :] = part[g].reshape(step * ROWS, LANES)
        return carry

    lax.fori_loop(0, CH // step, chunk, 0)
    emit_grads(scr, a_ref, p0_ref, p1_ref, ql_ref, qr_ref)


def hidden_kernel(pre_ref, c1_ref, c2_ref, mask_ref, h1_ref, h2_ref):
    step = 4
    mask = mask_ref[...].astype(F32)[None]
    for t, (c_ref, h_ref) in enumerate(((c1_ref, h1_ref), (c2_ref, h2_ref))):

        def chunk(j, carry):
            own = pl.ds(j * step, step)
            gout = sigmoid(pre_ref[t, pl.ds(2 * CH + j * step, step)].astype(F32))
            h_ref[own] = (mask * gout * jnp.tanh(c_ref[own])).astype(BF16)
            return carry

        lax.fori_loop(0, CH // step, chunk, 0)


def weights_kernel(k_ref, w_ref):
    for u in range(3):
        for v in range(3):
            tap = (3 * u + v) * W
            w_ref[u * W : (u + 1) * W, v * Q : (v + 1) * Q] = k_ref[:, tap : tap + W].astype(F32).T.astype(BF16)


def halo_rows(r0_ref, r1_ref, own):
    par = parity("row").astype(F32)
    low, high = edge_flags("row")
    first, second = r0_ref[own, :].astype(F32), r1_ref[own, :].astype(F32)
    above = second * ((1.0 - par) * low) + first * (par * low)
    below = first * ((1.0 - par) * high) + second * (par * high)
    return above, below


ZLANE = 16


def corner_kernel(with_z, r0_ref, r1_ref, ql_ref, qr_ref, c0_ref, c1_ref):
    par = parity("col").astype(F32)
    step = 32
    lanes = lane_ids(step)
    for k in range(Q // step):
        own = pl.ds(k * step, step)
        above, below = halo_rows(r0_ref, r1_ref, own)
        left = jnp.where(lanes == 0, above, ql_ref[own, :].astype(F32))
        left = jnp.where(lanes == SLABS - 1, pltpu.roll(below, SLABS - 1, 1), left)
        right = jnp.where(lanes == 0, pltpu.roll(above, 1, 1), qr_ref[own, :].astype(F32))
        right = jnp.where(lanes == SLABS - 1, pltpu.roll(below, SLABS, 1), right)
        if with_z and k < W // step:
            above, below = halo_rows(r0_ref, r1_ref, pl.ds(Q + k * step, step))
            far = ZLANE + SLABS - 1
            left = jnp.where(lanes == ZLANE, pltpu.roll(above, ZLANE, 1), left)
            left = jnp.where(lanes == far, pltpu.roll(below, far, 1), left)
            right = jnp.where(lanes == ZLANE, pltpu.roll(above, ZLANE + 1, 1), right)
            right = jnp.where(lanes == far, pltpu.roll(below, far + 1, 1), right)
        c0_ref[own, :] = (right * (1.0 - par) + left * par).astype(BF16)
        c1_ref[own, :] = (left * (1.0 - par) + right * par).astype(BF16)


def halo_columns(c0_ref, c1_ref, own):
    par = parity("col").astype(F32)
    low, high = edge_flags("col")
    first, second = c0_ref[own, :].astype(F32), c1_ref[own, :].astype(F32)
    left = second * ((1.0 - par) * low) + first * (par * low)
    right = first * ((1.0 - par) * high) + second * (par * high)
    return left, right


def z_edges_kernel(x_ref, h_ref, p0_ref, p1_ref, zl_ref, zr_ref, tmp):
    stack_fields(0, x_ref, h_ref, tmp)
    top = tmp[pl.ds(0, W, stride=ROWS), :].astype(BF16)
    bottom = tmp[pl.ds(ROWS - 1, W, stride=ROWS), :].astype(BF16)
    by_parity(parity("row"), top, bottom, p0_ref, p1_ref, 0)
    step = 32
    lanes = lane_ids(step)
    for k in range(W // step):
        zl = jnp.zeros((step, LANES), F32)
        zr = jnp.zeros((step, LANES), F32)
        for r in range(ROWS):
            row = tmp[pl.ds(k * step * ROWS + r, step, stride=ROWS), :]
            lane = ZLANE + r + 1
            zl = jnp.where(lanes == lane, pltpu.roll(row, lane, 1), zl)
            zr = jnp.where(lanes == lane, pltpu.roll(row, lane + 1, 1), zr)
        zl_ref[pl.ds(k * step, step), :] = zl.astype(BF16)
        zr_ref[pl.ds(k * step, step), :] = zr.astype(BF16)


def interior_kernel(a_ref, w_ref, b_ref, y_ref, y3):
    step = 32
    lanes = lane_ids(step)
    for k in range(Q // step):
        for r in range(ROWS):
            span = slice(r * LANES, (r + 1) * LANES)
            block = a_ref[pl.ds(k * step, step), span]
            row = block.astype(F32)
            minus = jnp.where(lanes == LANES - 1, 0.0, pltpu.roll(row, LANES - 1, 1))
            plus = jnp.where(lanes == 0, 0.0, pltpu.roll(row, 1, 1))
            b_ref[pl.ds(k * step, step), span] = minus.astype(BF16)
            b_ref[pl.ds(Q + k * step, step), span] = block
            b_ref[pl.ds(2 * Q + k * step, step), span] = plus.astype(BF16)
    y3[...] = lax.dot_general(w_ref[...], b_ref[...], (((1,), (0,)), ((), ())), preferred_element_type=F32)
    for r in range(ROWS):
        total = y3[W : 2 * W, r * LANES : (r + 1) * LANES]
        if r < ROWS - 1:
            total = total + y3[0:W, (r + 1) * LANES : (r + 2) * LANES]
        if r > 0:
            total = total + y3[2 * W : 3 * W, (r - 1) * LANES : r * LANES]
        y_ref[:, r * LANES : (r + 1) * LANES] = total


def build_halo(r0_ref, r1_ref, c0_ref, c1_ref, b_ref):
    step = 32
    lanes = lane_ids(step)
    inside = (lanes >= 1) & (lanes <= ROWS)
    last = SLABS - 1
    for k in range(Q // step):
        own = pl.ds(k * step, step)
        above, below = halo_rows(r0_ref, r1_ref, own)
        left, right = halo_columns(c0_ref, c1_ref, own)
        for n, (row, s) in enumerate(((above, 0), (below, last))):
            span = slice(n * LANES, (n + 1) * LANES)
            minus = jnp.where(lanes == LANES - 1, pltpu.roll(right, LANES - 1 - s, 1), pltpu.roll(row, LANES - 1, 1))
            plus = jnp.where(lanes == 0, pltpu.roll(left, (LANES - s) % LANES, 1), pltpu.roll(row, 1, 1))
            b_ref[pl.ds(k * step, step), span] = minus.astype(BF16)
            b_ref[pl.ds(Q + k * step, step), span] = row.astype(BF16)
            b_ref[pl.ds(2 * Q + k * step, step), span] = plus.astype(BF16)
        span = slice(2 * LANES, 3 * LANES)
        b_ref[pl.ds(k * step, step), span] = jnp.where(inside, right, 0.0).astype(BF16)
        b_ref[pl.ds(Q + k * step, step), span] = jnp.zeros((step, LANES), BF16)
        b_ref[pl.ds(2 * Q + k * step, step), span] = pltpu.roll(jnp.where(inside, left, 0.0), LANES // 2, 1).astype(BF16)


def finish_y(w_ref, b_ref, y_ref, y3, scr):
    y3[...] = lax.dot_general(w_ref[...], b_ref[...], (((1,), (0,)), ((), ())), preferred_element_type=F32)
    step = 32
    lanes = lane_ids(step)
    for k in range(W // step):
        side = 0.0
        for u in range(3):
            piece = y3[pl.ds(u * W + k * step, step), 2 * LANES :]
            side = side + (piece if u == 2 else pltpu.roll(piece, LANES + u - 2, 1))
        for r in range(ROWS):
            total = y_ref[pl.ds(k * step, step), r * LANES : (r + 1) * LANES]
            if r == 0:
                total = total + y3[pl.ds(2 * W + k * step, step), 0:LANES]
            if r == ROWS - 1:
                total = total + y3[pl.ds(k * step, step), LANES : 2 * LANES]
            right = jnp.where(lanes == LANES - 1, pltpu.roll(side, LANES - 1 - r, 1), 0.0)
            left = jnp.where(lanes == 0, pltpu.roll(side, LANES // 2 - r, 1), right)
            scr[pl.ds(k * step * ROWS + r, step, stride=ROWS), :] = total + left


def backward_kernel(t, with_z, *refs):
    edges = refs[:4] if with_z else None
    refs = refs[4:] if with_z else refs
    (r0_ref, r1_ref, k0_ref, k1_ref, w_ref, y_ref, pre_ref, cot_ref, before_ref, cell_ref, mask_ref, dc_in,
     gi_ref, b_ref, dc_ref, a_ref, p0_ref, p1_ref, ql_ref, qr_ref, y3, yscr, scr) = refs
    build_halo(r0_ref, r1_ref, k0_ref, k1_ref, b_ref)
    finish_y(w_ref, b_ref, y_ref, y3, yscr)
    step = 4
    mask = mask_ref[...].astype(F32)[None]

    def chunk(j, carry):
        base = j * step
        own = pl.ds(base, step)

        def gate(g):
            return pre_ref[t, pl.ds(g * CH + base, step)].astype(F32)

        gi_ref[own] = yscr[pl.ds(base * ROWS, step * ROWS), :].reshape(step, ROWS, LANES).astype(BF16)
        dh = yscr[pl.ds((CH + base) * ROWS, step * ROWS), :].reshape(step, ROWS, LANES)
        pre = (sigmoid(gate(0)), sigmoid(gate(1)), sigmoid(gate(2)), jnp.tanh(gate(3)))
        part = [None] * 4
        dc_ref[own] = gate_grads(pre, part, cot_ref[t, own].astype(F32), dh, mask, before_ref[own], jnp.tanh(cell_ref[own]), dc_in[own])
        for g in range(4):
            scr[pl.ds((g * CH + base) * ROWS, step * ROWS), :] = part[g].reshape(step * ROWS, LANES)
        return carry

    lax.fori_loop(0, CH // step, chunk, 0)
    emit_grads(scr, a_ref, p0_ref, p1_ref, ql_ref, qr_ref)
    if with_z:
        z0_ref, z1_ref, zl_ref, zr_ref = edges
        p0_ref[Q:, :] = z0_ref[...]
        p1_ref[Q:, :] = z1_ref[...]
        ql_ref[0:W, :] = (ql_ref[0:W, :].astype(F32) + zl_ref[...].astype(F32)).astype(BF16)
        qr_ref[0:W, :] = (qr_ref[0:W, :].astype(F32) + zr_ref[...].astype(F32)).astype(BF16)


def last_kernel(gi1_ref, gi2_ref, dc_ref, r0_ref, r1_ref, k0_ref, k1_ref, w_ref, y_ref, gi_ref, dh_ref, cell_ref, b_ref, y3, yscr):
    build_halo(r0_ref, r1_ref, k0_ref, k1_ref, b_ref)
    finish_y(w_ref, b_ref, y_ref, y3, yscr)
    gi_ref[0] = yscr[0 : CH * ROWS, :].reshape(CH, ROWS, LANES).astype(BF16)
    gi_ref[1] = gi1_ref[...]
    gi_ref[2] = gi2_ref[...]
    cell_ref[...] = dc_ref[...]
    dh_ref[...] = yscr[CH * ROWS :, :].reshape(CH, ROWS, LANES)


ZROWS = 3 * W + 16
CELLS = ROWS * LANES
CONTRACT_LANES = (((1,), (1,)), ((), ()))


def stack_fields(t, x_ref, h_ref, tmp):
    tmp[0 : CH * ROWS, :] = x_ref[t].astype(F32).reshape(CH * ROWS, LANES)
    tmp[CH * ROWS :, :] = h_ref[...].astype(F32).reshape(CH * ROWS, LANES)


def taps(z3, b_ref, bias):
    for v in range(3):
        span = ZROWS if bias and v == 1 else 3 * W
        got = lax.dot_general(z3[0:span, :], b_ref[v * Q : (v + 1) * Q, :], CONTRACT_LANES, preferred_element_type=F32)
        for u in range(3):
            yield u * 3 + v, got[u * W : (u + 1) * W]
        if bias and v == 1:
            yield 9, got[3 * W :]


def interior_taps(tmp, b_ref, z3):
    zero = jnp.zeros((W, LANES), BF16)
    z3[0:W, 0:LANES] = zero
    z3[2 * W : 3 * W, CELLS - LANES :] = zero
    for r in range(ROWS):
        row = tmp[pl.ds(r, W, stride=ROWS), :].astype(BF16)
        for u in range(3):
            n = r + 1 - u
            if 0 <= n < ROWS:
                z3[u * W : (u + 1) * W, n * LANES : (n + 1) * LANES] = row
    ids = lax.broadcasted_iota(jnp.int32, (16, CELLS), 0)
    z3[3 * W :, :] = jnp.where(ids == 0, 1.0, 0.0).astype(BF16)
    yield from taps(z3, b_ref, True)


def halo_taps(tmp, b_ref, zh):
    zero = jnp.zeros((W, LANES), BF16)
    zh[0:W, 0:LANES] = zero
    zh[W : 2 * W, 0:LANES] = zero
    zh[2 * W :, 0:LANES] = tmp[pl.ds(0, W, stride=ROWS), :].astype(BF16)
    zh[0:W, LANES : 2 * LANES] = tmp[pl.ds(ROWS - 1, W, stride=ROWS), :].astype(BF16)
    zh[W : 2 * W, LANES : 2 * LANES] = zero
    zh[2 * W :, LANES : 2 * LANES] = zero
    step = 32
    lanes = lane_ids(step)
    half = LANES // 2
    for k in range(W // step):
        side = jnp.zeros((step, LANES), F32)
        for r in range(ROWS):
            row = tmp[pl.ds(k * step * ROWS + r, step, stride=ROWS), :]
            side = jnp.where(lanes == r, pltpu.roll(row, r + 1, 1), side)
            side = jnp.where(lanes == half + r, pltpu.roll(row, half + r, 1), side)
        for u in range(3):
            zh[pl.ds(u * W + k * step, step), 2 * LANES :] = (side if u == 2 else pltpu.roll(side, 2 - u, 1)).astype(BF16)
    yield from taps(zh, b_ref, False)


def accumulate_kernel(t, has_acc, with_halo, *refs):
    refs = list(refs)
    acc_ref = refs.pop(0) if has_acc else None
    x_ref, h_ref, b_ref = refs[:3]
    out_ref, z3, zh, tmp = refs[-4:]
    stack_fields(t, x_ref, h_ref, tmp)
    for tap, got in interior_taps(tmp, b_ref, z3):
        rows = slice(tap * W, tap * W + got.shape[0])
        out_ref[rows, :] = acc_ref[rows, :] + got if has_acc else got
    if with_halo:
        for tap, got in halo_taps(tmp, refs[3], zh):
            rows = slice(tap * W, tap * W + got.shape[0])
            out_ref[rows, :] += got


def z_windows(tmp, r0_ref, r1_ref, k0_ref, k1_ref, zw):
    step = 32
    lanes = lane_ids(step)
    for k in range(W // step):
        above, below = halo_rows(r0_ref, r1_ref, pl.ds(Q + k * step, step))
        left, right = halo_columns(k0_ref, k1_ref, pl.ds(k * step, step))
        for source in range(-1, ROWS + 1):
            if source < 0:
                row = above
            elif source == ROWS:
                row = below
            else:
                row = tmp[pl.ds(k * step * ROWS + source, step, stride=ROWS), :]
            lane = ZLANE + source + 1
            shifted = (
                jnp.where(lanes == 0, pltpu.roll(left, LANES - lane, 1), pltpu.roll(row, 1, 1)),
                row,
                jnp.where(lanes == LANES - 1, pltpu.roll(right, LANES - 1 - lane, 1), pltpu.roll(row, LANES - 1, 1)),
            )
            for v in range(3):
                block = shifted[v].astype(BF16)
                for u in range(3):
                    r = source - (u - 1)
                    if 0 <= r < ROWS:
                        zw[pl.ds((3 * u + v) * W + k * step, step), r * LANES : (r + 1) * LANES] = block
    ids = lax.broadcasted_iota(jnp.int32, (16, CELLS), 0)
    zw[9 * W :, :] = jnp.where(ids == 0, 1.0, 0.0).astype(BF16)


def send_kernel(blocks, scale, acc_ref, x_ref, h2_ref, b_ref, h_ref, r0_ref, r1_ref, k0_ref, k1_ref, a_ref, out_ref, zh, zw, tmp, total):
    stack_fields(0, x_ref, h_ref, tmp)
    z_windows(tmp, r0_ref, r1_ref, k0_ref, k1_ref, zw)
    total[...] = acc_ref[...] + lax.dot_general(zw[...], a_ref[...], CONTRACT_LANES, preferred_element_type=F32)
    stack_fields(1, x_ref, h2_ref, tmp)
    for tap, got in halo_taps(tmp, b_ref, zh):
        rows = slice(tap * W, tap * W + got.shape[0])
        total[rows, :] += got
    bias = total[9 * W : 9 * W + 8, :] * scale
    high = jnp.broadcast_to(bias[0:1], (8, Q)).astype(BF16).astype(F32)
    low = jnp.broadcast_to(bias[0:1], (8, Q)) - high
    ids = lax.broadcasted_iota(jnp.int32, (8, Q), 0)
    tail = jnp.where(ids == 0, high, jnp.where(ids == 1, low, 0.0))
    size = 9 * W // blocks
    for c in range(blocks):
        body = jnp.concatenate([total[c * size : (c + 1) * size, :] * scale, tail], axis=0)
        out_ref[c * (size + 8) : (c + 1) * (size + 8), :] = body.astype(BF16)


def result_kernel(blocks, in_ref, k_ref, bias_ref, scr):
    size = in_ref.shape[0] // blocks
    total = in_ref[0:size, :]
    for c in range(1, blocks):
        total = total + in_ref[c * size : (c + 1) * size, :]
    taps_here = k_ref.shape[1]
    k_ref[...] = total[:, 0:taps_here]
    scr[...] = jnp.broadcast_to(total[:, taps_here : taps_here + 1] + total[:, taps_here + 1 : taps_here + 2], scr.shape)
    count = bias_ref.shape[0]
    bias_ref[...] = scr[pl.ds(lax.axis_index("col") * count, count), 0:1]


def fold_kernel(blocks, in_ref, out_ref):
    size = in_ref.shape[0] // blocks
    total = in_ref[0:size, :].astype(F32)
    for c in range(1, blocks):
        total = total + in_ref[c * size : (c + 1) * size, :].astype(F32)
    out_ref[...] = total.T


def even_swap(count):
    return [(i, i ^ 1) for i in range(count)]


def odd_swap(count):
    return [(i, (i + 1) % count if i % 2 else (i - 1) % count) for i in range(count)]


def swaps(first, second, axis):
    count = lax.axis_size(axis)
    return lax.ppermute(first, axis, even_swap(count)), lax.ppermute(second, axis, odd_swap(count))


def struct(shape, dtype):
    return jax.ShapeDtypeStruct(shape, dtype)


def shards(inputs, gate_pre, cotangent, hidden_init, cell_init, land_mask, kernel):
    field = (CH, ROWS, LANES)
    nrow, ncol = lax.axis_size("row"), lax.axis_size("col")
    scale = 1.0 / math.sqrt(ROWS * LANES * nrow * ncol)
    edge = struct((Q, LANES), BF16)
    grads_out = (struct((Q, CELLS), BF16), edge, edge, edge, edge)
    scr = pltpu.VMEM((Q * ROWS, LANES), F32)
    y3 = pltpu.VMEM((3 * W, 3 * LANES), F32)
    tmp = pltpu.VMEM((W * ROWS, LANES), F32)
    z3, zh = pltpu.VMEM((ZROWS, CELLS), BF16), pltpu.VMEM((3 * W, 3 * LANES), BF16)
    hbm = pl.BlockSpec(memory_space=pltpu.MemorySpace.HBM)

    c1, c2, dc, a, p0, p1, ql, qr = call(
        forward_kernel,
        (struct(field, F32), struct(field, F32), struct(field, F32)) + grads_out,
        in_specs=[hbm] * 4,
        out_specs=[whole()] * 8,
        scratch=[
            scr,
            pltpu.VMEM((3, Q, ROWS, LANES), BF16),
            pltpu.VMEM(field, BF16),
            pltpu.VMEM(field, F32),
            pltpu.VMEM((ROWS, LANES), jnp.int32),
            pltpu.SemaphoreType.DMA((13,)),
        ],
    )(*(in_hbm(x) for x in (gate_pre, cotangent, cell_init, land_mask)))

    h1, h2 = call(hidden_kernel, (struct(field, BF16),) * 2, in_specs=[whole()] * 4, out_specs=[whole()] * 2)(gate_pre, c1, c2, land_mask)
    cells = [cell_init, c1, c2]
    hiddens = [hidden_init, h1, h2]
    interior, halo = struct((3 * Q, CELLS), BF16), struct((3 * Q, 3 * LANES), BF16)
    acc_shape = struct((9 * W + 16, Q), F32)

    def corner(with_z, r0, r1, ql, qr):
        out = call(functools.partial(corner_kernel, with_z), (edge, edge), in_specs=[whole()] * 4, out_specs=[whole()] * 2)
        return out(r0, r1, ql, qr)

    def inside(a):
        return call(
            interior_kernel,
            (interior, struct((W, CELLS), F32)),
            in_specs=[whole()] * 2,
            out_specs=[whole()] * 2,
            scratch=[pltpu.VMEM((3 * W, CELLS), F32)],
        )(a, weights)

    def backward(t, edges, r0, r1, k0, k1, y, dc):
        pay = struct((Q + W, LANES), BF16) if edges else edge
        return call(
            functools.partial(backward_kernel, t - 1, bool(edges)),
            (struct(field, BF16), halo, struct(field, F32), struct((Q, CELLS), BF16), pay, pay, edge, edge),
            in_specs=[whole()] * (len(edges) + 12),
            out_specs=[whole()] * 8,
            scratch=[y3, tmp, scr],
        )(*edges, r0, r1, k0, k1, weights, y, gate_pre, cotangent, cells[t - 1], cells[t], land_mask, dc)

    def accumulate(t, acc, b, bh):
        head = [] if acc is None else [acc]
        rest = [b] if bh is None else [b, bh]
        return call(
            functools.partial(accumulate_kernel, t, acc is not None, bh is not None),
            acc_shape,
            in_specs=[whole()] * (len(head) + 2 + len(rest)),
            out_specs=whole(),
            scratch=[z3, zh, tmp],
            aliases={0: 0} if head else {},
        )(*head, inputs, hiddens[t], *rest)

    r0, r1 = swaps(p0, p1, "row")
    weights = call(weights_kernel, struct((3 * W, 3 * Q), BF16), in_specs=[whole()], out_specs=whole())(kernel)
    zedge = struct((W, LANES), BF16)
    edges = call(
        z_edges_kernel, (zedge,) * 4, in_specs=[whole()] * 2, out_specs=[whole()] * 4, scratch=[tmp]
    )(inputs, hidden_init)
    r0, r1, weights, edges = lax.optimization_barrier((r0, r1, weights, edges))
    k0, k1 = swaps(*corner(False, r0, r1, ql, qr), "col")
    b, y = inside(a)
    gi2, bh, dc, a, p0, p1, ql, qr = backward(2, edges, r0, r1, k0, k1, y, dc)
    r0, r1 = swaps(p0, p1, "row")
    acc = accumulate(2, None, b, bh)
    r0, r1, acc = lax.optimization_barrier((r0, r1, acc))
    k0, k1 = swaps(*corner(True, r0, r1, ql, qr), "col")
    b, y = inside(a)
    acc = accumulate(1, acc, b, None)
    gi1, bh, dc, a, p0, p1, ql, qr = backward(1, [], r0, r1, k0, k1, y, dc)
    size = 9 * W // ncol + 8
    send = call(
        functools.partial(send_kernel, ncol, scale),
        struct((ncol * size, Q), BF16),
        in_specs=[whole()] * 10,
        out_specs=whole(),
        scratch=[zh, pltpu.VMEM((9 * W + 16, CELLS), BF16), tmp, pltpu.VMEM((9 * W + 16, Q), F32)],
    )(acc, inputs, hiddens[1], bh, hiddens[0], r0, r1, k0, k1, a)
    r0, r1 = swaps(p0, p1, "row")
    got = lax.all_to_all(send, "col", 0, 0, tiled=True)
    c0, c1 = corner(False, r0, r1, ql, qr)
    k0, k1 = swaps(c0, c1, "col")
    b, y = inside(a)
    got, c0, y = lax.optimization_barrier((got, c0, y))
    folded = call(functools.partial(fold_kernel, ncol), struct((Q, size), F32), in_specs=[whole()], out_specs=whole())(got)
    got = lax.all_to_all(folded, "row", 0, 0, tiled=True)
    y, folded = lax.optimization_barrier((y, folded))
    gi, grad_hidden, grad_cell = call(
        last_kernel,
        (struct((3,) + field, BF16), struct(field, F32), struct(field, F32)),
        in_specs=[whole()] * 9,
        out_specs=[whole()] * 3,
        scratch=[pltpu.VMEM((3 * Q, 3 * LANES), BF16), y3, tmp],
    )(gi1, gi2, dc, r0, r1, k0, k1, weights, y)
    count = Q // nrow // ncol
    grad_kernel, grad_bias = call(
        functools.partial(result_kernel, nrow),
        (struct((Q // nrow, size - 8), F32), struct((count, 1), F32)),
        in_specs=[whole()],
        out_specs=[whole()] * 2,
        scratch=[pltpu.VMEM((Q // nrow, LANES), F32)],
    )(got)
    return (gi, grad_hidden, grad_cell, grad_kernel, grad_bias.reshape(count))


def solution(mesh):
    placed = (
        P(None, None, "row", "col"),
        P(None, None, "row", "col"),
        P(None, None, "row", "col"),
        P(None, "row", "col"),
        P(None, "row", "col"),
        P("row", "col"),
        P(),
    )
    return jax.shard_map(
        shards,
        mesh=mesh,
        in_specs=placed,
        out_specs=(
            P(None, None, "row", "col"),
            P(None, "row", "col"),
            P(None, "row", "col"),
            P("row", "col"),
            P(("row", "col")),
        ),
        check_vma=False,
    )
```

```python
import functools
import math

import jax
import jax.numpy as jnp
from jax import lax
from jax.experimental import pallas as pl
from jax.experimental.pallas import tpu as pltpu
from jax.sharding import PartitionSpec as P

INTERPRET = False
VMEM_LIMIT = 24 << 20
F32 = jnp.float32
BF16 = jnp.bfloat16
ROWS = 8
LANES = 128
SLABS = ROWS + 2
CH = 64
Q = 4 * CH
W = 2 * CH


def call(body, out_shape, in_specs=None, out_specs=None, scratch=(), aliases=None):
    kwargs = {}
    if in_specs is not None:
        kwargs["in_specs"] = in_specs
    if out_specs is not None:
        kwargs["out_specs"] = out_specs
    return pl.pallas_call(
        body,
        out_shape=out_shape,
        scratch_shapes=list(scratch),
        input_output_aliases=aliases or {},
        interpret=INTERPRET,
        grid=(1,),
        compiler_params=pltpu.CompilerParams(vmem_limit_bytes=VMEM_LIMIT),
        **kwargs,
    )


def whole():
    return pl.BlockSpec(memory_space=pltpu.VMEM)


def in_hbm(x):
    return x if INTERPRET else pltpu.with_memory_space_constraint(x, pltpu.MemorySpace.HBM)


def sigmoid(x):
    return 0.5 * jnp.tanh(0.5 * x) + 0.5


def lane_ids(rows):
    return lax.broadcasted_iota(jnp.int32, (rows, LANES), 1)


def parity(axis):
    return lax.rem(lax.axis_index(axis), 2)


def edge_flags(axis):
    index = lax.axis_index(axis)
    low = jnp.where(index > 0, 1.0, 0.0).astype(F32)
    high = jnp.where(index < lax.axis_size(axis) - 1, 1.0, 0.0).astype(F32)
    return low, high


def gate_grads(pre, part, cot, dh, mask, cell_before, tanh_cell, dc):
    gin, gfor, gout, gcand = pre
    error = mask * (cot if dh is None else dh + cot)
    eo = error * gout
    grad = eo * (1.0 - tanh_cell * tanh_cell)
    if dc is not None:
        grad = dc + grad
    gi = grad * gin
    part[0] = gi * gcand * (1.0 - gin)
    df = grad * gfor
    part[1] = df * cell_before * (1.0 - gfor)
    part[2] = eo * tanh_cell * (1.0 - gout)
    part[3] = gi * (1.0 - gcand * gcand)
    return df


def by_parity(par, top, bottom, p0_ref, p1_ref, start):
    rows = slice(start, start + top.shape[0])

    @pl.when(par == 0)
    def _():
        p0_ref[rows, :] = bottom
        p1_ref[rows, :] = top

    @pl.when(par == 1)
    def _():
        p0_ref[rows, :] = top
        p1_ref[rows, :] = bottom


def emit_grads(scr, a_ref, p0_ref, p1_ref, packs=None):
    step = 32
    lanes = lane_ids(step)
    for k in range(Q // step):
        own = pl.ds(k * step, step)
        ql = jnp.zeros((step, LANES), F32)
        qr = jnp.zeros((step, LANES), F32)
        for r in range(ROWS):
            row = scr[pl.ds(k * step * ROWS + r, step, stride=ROWS), :]
            a_ref[own, r * LANES : (r + 1) * LANES] = row.astype(BF16)
            if packs:
                ql = jnp.where(lanes == r + 1, pltpu.roll(row, r + 1, 1), ql)
                qr = jnp.where(lanes == r + 1, pltpu.roll(row, r + 2, 1), qr)
        if packs:
            packs[0][own, :] = ql.astype(BF16)
            packs[1][own, :] = qr.astype(BF16)
    by_parity(parity("row"), a_ref[:, 0:LANES], a_ref[:, (ROWS - 1) * LANES :], p0_ref, p1_ref, 0)


def forward_kernel(pre_hbm, cot_hbm, c0_hbm, mask_hbm, c1_ref, c2_ref, dc_ref, a_ref, p0_ref, p1_ref, scr, pre_ref, cot_ref, c0_ref, mask_ref, sems):
    pairs = [(c0_hbm, c0_ref), (mask_hbm, mask_ref), (cot_hbm.at[2], cot_ref)]
    for t, g in ((0, 1), (0, 0), (0, 3), (1, 1), (1, 0), (1, 3), (2, 1), (2, 0), (2, 3), (2, 2)):
        own = pl.ds(g * CH, CH)
        pairs.append((pre_hbm.at[t, own], pre_ref.at[t, own]))
    copies = [pltpu.make_async_copy(src, dst, sems.at[n]) for n, (src, dst) in enumerate(pairs)]
    order = [3, 4, 0, 5, 6, 7, 8, 9, 10, 11, 12, 2, 1]
    for n in order:
        copies[n].start()
    step = 4

    def gate(t, g, base):
        return pre_ref[t, pl.ds(g * CH + base, step)].astype(F32)

    copies[0].wait()
    for t, (before_ref, c_ref) in enumerate(((c0_ref, c1_ref), (c1_ref, c2_ref))):
        for n in range(3 + 3 * t, 6 + 3 * t):
            copies[n].wait()

        def advance(j, carry):
            base = j * step
            own = pl.ds(base, step)
            c_ref[own] = sigmoid(gate(t, 1, base)) * before_ref[own] + sigmoid(gate(t, 0, base)) * jnp.tanh(gate(t, 3, base))
            return carry

        lax.fori_loop(0, CH // step, advance, 0)
    for n in (9, 10, 11, 12, 2, 1):
        copies[n].wait()
    mask = mask_ref[...].astype(F32)[None]

    def chunk(j, carry):
        base = j * step
        own = pl.ds(base, step)
        cell = c2_ref[own]
        pre = (sigmoid(gate(2, 0, base)), sigmoid(gate(2, 1, base)), sigmoid(gate(2, 2, base)), jnp.tanh(gate(2, 3, base)))
        tanh_cell = jnp.tanh(pre[1] * cell + pre[0] * pre[3])
        part = [None] * 4
        dc_ref[own] = gate_grads(pre, part, cot_ref[own].astype(F32), None, mask, cell, tanh_cell, None)
        for g in range(4):
            scr[pl.ds((g * CH + base) * ROWS, step * ROWS), :] = part[g].reshape(step * ROWS, LANES)
        return carry

    lax.fori_loop(0, CH // step, chunk, 0)
    emit_grads(scr, a_ref, p0_ref, p1_ref)


def hidden_kernel(pre_ref, c1_ref, c2_ref, mask_ref, h1_ref, h2_ref):
    step = 4
    mask = mask_ref[...].astype(F32)[None]
    for t, (c_ref, h_ref) in enumerate(((c1_ref, h1_ref), (c2_ref, h2_ref))):

        def chunk(j, carry):
            own = pl.ds(j * step, step)
            gout = sigmoid(pre_ref[t, pl.ds(2 * CH + j * step, step)].astype(F32))
            h_ref[own] = (mask * gout * jnp.tanh(c_ref[own])).astype(BF16)
            return carry

        lax.fori_loop(0, CH // step, chunk, 0)


def weights_kernel(k_ref, w_ref):
    for u in range(3):
        for v in range(3):
            tap = (3 * u + v) * W
            w_ref[u * W : (u + 1) * W, v * Q : (v + 1) * Q] = k_ref[:, tap : tap + W].astype(F32).T.astype(BF16)


def halo_rows(r0_ref, r1_ref, own):
    par = parity("row").astype(F32)
    low, high = edge_flags("row")
    first, second = r0_ref[own, :].astype(F32), r1_ref[own, :].astype(F32)
    above = second * ((1.0 - par) * low) + first * (par * low)
    below = first * ((1.0 - par) * high) + second * (par * high)
    return above, below


SECOND, PRE, STATE, ZLANE = 16, 32, 48, 64
CORNER = Q + W


def move(x, source, target):
    shift = (target - source) % LANES
    return pltpu.roll(x, shift, 1) if shift else x


def corner_kernel(wide, r0_ref, r1_ref, ql_ref, qr_ref, c0_ref, c1_ref):
    par = parity("col").astype(F32)
    step = 32
    lanes = lane_ids(step)
    for k in range(Q // step):
        own = pl.ds(k * step, step)
        above, below = halo_rows(r0_ref, r1_ref, own)
        left, right = ql_ref[own, :].astype(F32), qr_ref[own, :].astype(F32)
        for depth in range(2 if wide else 1):
            for row, lane in ((above, depth * SECOND), (below, depth * SECOND + SLABS - 1)):
                left = jnp.where(lanes == lane, move(row, depth, lane), left)
                right = jnp.where(lanes == lane, move(row, LANES - 1 - depth, lane), right)
        c0_ref[own, :] = (right * (1.0 - par) + left * par).astype(BF16)
        c1_ref[own, :] = (left * (1.0 - par) + right * par).astype(BF16)


def halo_columns(c0_ref, c1_ref, own):
    par = parity("col").astype(F32)
    low, high = edge_flags("col")
    first, second = c0_ref[own, :].astype(F32), c1_ref[own, :].astype(F32)
    left = second * ((1.0 - par) * low) + first * (par * low)
    right = first * ((1.0 - par) * high) + second * (par * high)
    return left, right


def edges_kernel(a_ref, pre_ref, cot_ref, cell_ref, dc_ref, mask_ref, x_ref, h_ref, p0_ref, p1_ref, ql_ref, qr_ref, pre_tmp, state, tmp):
    stack_fields(0, x_ref, h_ref, tmp)
    top = tmp[pl.ds(0, W, stride=ROWS), :].astype(BF16)
    bottom = tmp[pl.ds(ROWS - 1, W, stride=ROWS), :].astype(BF16)
    by_parity(parity("row"), top, bottom, p0_ref, p1_ref, 0)
    land = mask_ref[...][None] > 0
    size = CH * ROWS
    for g in range(4):
        block = pre_ref[1, g * CH : (g + 1) * CH].astype(F32)
        if g == 2:
            block = jnp.where(land, block, -64.0)
        pre_tmp[g * size : (g + 1) * size, :] = block.reshape(size, LANES)
    state[0:size, :] = cot_ref[1].astype(F32).reshape(size, LANES)
    state[size : 2 * size, :] = cell_ref[...].reshape(size, LANES)
    state[2 * size :, :] = dc_ref[...].reshape(size, LANES)
    step = 32
    lanes = lane_ids(step)
    for k in range(Q // step):
        left = jnp.zeros((step, LANES), F32)
        right = jnp.zeros((step, LANES), F32)
        for r in range(ROWS):
            own = pl.ds(k * step * ROWS + r, step, stride=ROWS)
            row = a_ref[pl.ds(k * step, step), r * LANES : (r + 1) * LANES].astype(F32)
            pieces = [(row, 0, 0), (row, 1, SECOND), (pre_tmp[own, :], 0, PRE)]
            if k < 3 * CH // step:
                pieces.append((state[own, :], 0, STATE))
            if k < W // step:
                pieces.append((tmp[own, :], 0, ZLANE))
            for piece, depth, slot in pieces:
                lane = slot + r + 1
                left = jnp.where(lanes == lane, move(piece, depth, lane), left)
                right = jnp.where(lanes == lane, move(piece, LANES - 1 - depth, lane), right)
        ql_ref[pl.ds(k * step, step), :] = left.astype(BF16)
        qr_ref[pl.ds(k * step, step), :] = right.astype(BF16)


def interior_kernel(a_ref, w_ref, b_ref, y_ref, y3):
    step = 32
    lanes = lane_ids(step)
    for k in range(Q // step):
        for r in range(ROWS):
            span = slice(r * LANES, (r + 1) * LANES)
            block = a_ref[pl.ds(k * step, step), span]
            row = block.astype(F32)
            minus = jnp.where(lanes == LANES - 1, 0.0, pltpu.roll(row, LANES - 1, 1))
            plus = jnp.where(lanes == 0, 0.0, pltpu.roll(row, 1, 1))
            b_ref[pl.ds(k * step, step), span] = minus.astype(BF16)
            b_ref[pl.ds(Q + k * step, step), span] = block
            b_ref[pl.ds(2 * Q + k * step, step), span] = plus.astype(BF16)
    y3[...] = lax.dot_general(w_ref[...], b_ref[...], (((1,), (0,)), ((), ())), preferred_element_type=F32)
    for r in range(ROWS):
        total = y3[W : 2 * W, r * LANES : (r + 1) * LANES]
        if r < ROWS - 1:
            total = total + y3[0:W, (r + 1) * LANES : (r + 2) * LANES]
        if r > 0:
            total = total + y3[2 * W : 3 * W, (r - 1) * LANES : r * LANES]
        y_ref[:, r * LANES : (r + 1) * LANES] = total


def travelled(r0_ref, r1_ref, c0_ref, c1_ref):
    def source(k, step):
        own = pl.ds(k * step, step)
        return halo_rows(r0_ref, r1_ref, own) + halo_columns(c0_ref, c1_ref, own)

    return source


def corner_lanes(lanes, r0_ref, r1_ref, group, left, right, first):
    above, below = halo_rows(r0_ref, r1_ref, pl.ds(CORNER, 32))
    for row, lane in ((above, first), (below, first + SLABS - 1)):
        right = jnp.where(lanes == lane, move(row, 2 * group, lane), right)
        left = jnp.where(lanes == lane, move(row, 2 * group + 1, lane), left)
    return left, right


def computed(r0_ref, r1_ref, pack_ref):
    def source(k, step):
        own = pl.ds(k * step, step)
        pack = pack_ref[own, :].astype(F32)
        columns = corner_lanes(lane_ids(step), r0_ref, r1_ref, k, pltpu.roll(pack, LANES // 2, 1), pack, 0)
        return halo_rows(r0_ref, r1_ref, own) + columns

    return source


def build_halo(source, b_ref):
    step = 32
    lanes = lane_ids(step)
    inside = (lanes >= 1) & (lanes <= ROWS)
    last = SLABS - 1
    for k in range(Q // step):
        above, below, left, right = source(k, step)
        for n, (row, s) in enumerate(((above, 0), (below, last))):
            span = slice(n * LANES, (n + 1) * LANES)
            minus = jnp.where(lanes == LANES - 1, pltpu.roll(right, LANES - 1 - s, 1), pltpu.roll(row, LANES - 1, 1))
            plus = jnp.where(lanes == 0, pltpu.roll(left, (LANES - s) % LANES, 1), pltpu.roll(row, 1, 1))
            b_ref[pl.ds(k * step, step), span] = minus.astype(BF16)
            b_ref[pl.ds(Q + k * step, step), span] = row.astype(BF16)
            b_ref[pl.ds(2 * Q + k * step, step), span] = plus.astype(BF16)
        span = slice(2 * LANES, 3 * LANES)
        b_ref[pl.ds(k * step, step), span] = jnp.where(inside, right, 0.0).astype(BF16)
        b_ref[pl.ds(Q + k * step, step), span] = jnp.zeros((step, LANES), BF16)
        b_ref[pl.ds(2 * Q + k * step, step), span] = pltpu.roll(jnp.where(inside, left, 0.0), LANES // 2, 1).astype(BF16)


def finish_y(w_ref, b_ref, y_ref, y3, scr):
    y3[...] = lax.dot_general(w_ref[...], b_ref[...], (((1,), (0,)), ((), ())), preferred_element_type=F32)
    step = 32
    lanes = lane_ids(step)
    for k in range(W // step):
        side = 0.0
        for u in range(3):
            piece = y3[pl.ds(u * W + k * step, step), 2 * LANES : 3 * LANES]
            side = side + (piece if u == 2 else pltpu.roll(piece, LANES + u - 2, 1))
        for r in range(ROWS):
            total = y_ref[pl.ds(k * step, step), r * LANES : (r + 1) * LANES]
            if r == 0:
                total = total + y3[pl.ds(2 * W + k * step, step), 0:LANES]
            if r == ROWS - 1:
                total = total + y3[pl.ds(k * step, step), LANES : 2 * LANES]
            right = jnp.where(lanes == LANES - 1, pltpu.roll(side, LANES - 1 - r, 1), 0.0)
            left = jnp.where(lanes == 0, pltpu.roll(side, LANES // 2 - r, 1), right)
            scr[pl.ds(k * step * ROWS + r, step, stride=ROWS), :] = total + left


def step_grads(t, pre_ref, cot_ref, before_ref, cell_ref, mask_ref, dc_in, gi_ref, dc_ref, yscr, scr):
    step = 4
    mask = mask_ref[...].astype(F32)[None]

    def chunk(j, carry):
        base = j * step
        own = pl.ds(base, step)

        def gate(g):
            return pre_ref[t, pl.ds(g * CH + base, step)].astype(F32)

        gi_ref[own] = yscr[pl.ds(base * ROWS, step * ROWS), :].reshape(step, ROWS, LANES).astype(BF16)
        dh = yscr[pl.ds((CH + base) * ROWS, step * ROWS), :].reshape(step, ROWS, LANES)
        pre = (sigmoid(gate(0)), sigmoid(gate(1)), sigmoid(gate(2)), jnp.tanh(gate(3)))
        part = [None] * 4
        dc_ref[own] = gate_grads(pre, part, cot_ref[t, own].astype(F32), dh, mask, before_ref[own], jnp.tanh(cell_ref[own]), dc_in[own])
        for g in range(4):
            scr[pl.ds((g * CH + base) * ROWS, step * ROWS), :] = part[g].reshape(step * ROWS, LANES)
        return carry

    lax.fori_loop(0, CH // step, chunk, 0)


def third_kernel(r0_ref, r1_ref, k0_ref, k1_ref, s0_ref, s1_ref, z0_ref, z1_ref, w_ref, y_ref, pre_ref, cot_ref, before_ref, cell_ref, mask_ref, dc_in,
                 gi_ref, bh_ref, dc_ref, a_ref, p0_ref, p1_ref, pack_ref, b_ref, y3, yscr, scr):
    build_halo(travelled(r0_ref, r1_ref, k0_ref, k1_ref), b_ref)
    par = parity("col").astype(F32)
    step = 32
    half = LANES // 2
    lanes = lane_ids(step)
    first, second = lanes < SLABS, (lanes >= half) & (lanes < half + SLABS)
    for k in range(Q // step):
        own = pl.ds(k * step, step)
        left, right = halo_columns(k0_ref, k1_ref, own)
        sent0, sent1 = s0_ref[own, :].astype(F32), s1_ref[own, :].astype(F32)
        my_right = sent0 * (1.0 - par) + sent1 * par
        my_left = sent1 * (1.0 - par) + sent0 * par
        pairs = (
            (move(right, SECOND, 0), move(my_left, 0, half)),
            (right, move(left, 0, half)),
            (my_right, move(left, SECOND, half)),
        )
        for v, (low, high) in enumerate(pairs):
            b_ref[pl.ds(v * Q + k * step, step), 3 * LANES :] = jnp.where(first, low, jnp.where(second, high, 0.0)).astype(BF16)
    bh_ref[...] = b_ref[:, 0 : 3 * LANES]
    finish_y(w_ref, b_ref, y_ref, y3, yscr)
    step_grads(1, pre_ref, cot_ref, before_ref, cell_ref, mask_ref, dc_in, gi_ref, dc_ref, yscr, scr)
    low, high = edge_flags("col")
    valid = jnp.where((lanes >= 1) & (lanes <= ROWS), high, jnp.where((lanes > half) & (lanes <= half + ROWS), low, 0.0))
    for j in range(CH // step):

        def border(start, slot):
            left, right = halo_columns(k0_ref, k1_ref, pl.ds(start + j * step, step))
            return jnp.where(lanes < half, move(right, slot, 0), move(left, slot, half))

        dh = 0.0
        for u in range(3):
            dh = dh + move(y3[pl.ds(u * W + CH + j * step, step), 3 * LANES :], 1, u)
        gates = [border(g * CH, PRE) for g in range(4)]
        cot, before, dc = (border(m * CH, STATE) for m in range(3))
        pre = (sigmoid(gates[0]), sigmoid(gates[1]), sigmoid(gates[2]), jnp.tanh(gates[3]))
        tanh_cell = jnp.tanh(pre[1] * before + pre[0] * pre[3])
        part = [None] * 4
        gate_grads(pre, part, cot, dh, valid, before, tanh_cell, dc * valid)
        for g in range(4):
            pack_ref[pl.ds(g * CH + j * step, step), :] = part[g].astype(BF16)
    emit_grads(scr, a_ref, p0_ref, p1_ref)
    p0_ref[Q:CORNER, :] = z0_ref[...]
    p1_ref[Q:CORNER, :] = z1_ref[...]
    corners = []
    for r in (0, ROWS - 1):
        block = jnp.zeros((step, LANES), F32)
        for k in range(Q // step):
            pack = pack_ref[pl.ds(k * step, step), :].astype(F32)
            block = jnp.where(lanes == 2 * k, move(pack, r + 1, 2 * k), block)
            block = jnp.where(lanes == 2 * k + 1, move(pack, half + r + 1, 2 * k + 1), block)
        for k in range(W // step):
            left, right = halo_columns(k0_ref, k1_ref, pl.ds(k * step, step))
            lane = 2 * (Q // step + k)
            block = jnp.where(lanes == lane, move(right, ZLANE + r + 1, lane), block)
            block = jnp.where(lanes == lane + 1, move(left, ZLANE + r + 1, lane + 1), block)
        corners.append(block.astype(BF16))
    by_parity(parity("row"), corners[0], corners[1], p0_ref, p1_ref, CORNER)


def second_kernel(r0_ref, r1_ref, pack_ref, w_ref, y_ref, pre_ref, cot_ref, before_ref, cell_ref, mask_ref, dc_in,
                  gi_ref, b_ref, dc_ref, a_ref, p0_ref, p1_ref, ql_ref, qr_ref, y3, yscr, scr):
    build_halo(computed(r0_ref, r1_ref, pack_ref), b_ref)
    finish_y(w_ref, b_ref, y_ref, y3, yscr)
    step_grads(0, pre_ref, cot_ref, before_ref, cell_ref, mask_ref, dc_in, gi_ref, dc_ref, yscr, scr)
    emit_grads(scr, a_ref, p0_ref, p1_ref, (ql_ref, qr_ref))


def last_kernel(gi1_ref, gi2_ref, dc_ref, r0_ref, r1_ref, k0_ref, k1_ref, w_ref, y_ref, gi_ref, dh_ref, cell_ref, b_ref, y3, yscr):
    build_halo(travelled(r0_ref, r1_ref, k0_ref, k1_ref), b_ref)
    finish_y(w_ref, b_ref, y_ref, y3, yscr)
    gi_ref[0] = yscr[0 : CH * ROWS, :].reshape(CH, ROWS, LANES).astype(BF16)
    gi_ref[1] = gi1_ref[...]
    gi_ref[2] = gi2_ref[...]
    cell_ref[...] = dc_ref[...]
    dh_ref[...] = yscr[CH * ROWS :, :].reshape(CH, ROWS, LANES)


ZROWS = 3 * W + 16
CELLS = ROWS * LANES
CONTRACT_LANES = (((1,), (1,)), ((), ()))


def stack_fields(t, x_ref, h_ref, tmp):
    tmp[0 : CH * ROWS, :] = x_ref[t].astype(F32).reshape(CH * ROWS, LANES)
    tmp[CH * ROWS :, :] = h_ref[...].astype(F32).reshape(CH * ROWS, LANES)


def taps(z3, b_ref, bias):
    for v in range(3):
        span = ZROWS if bias and v == 1 else 3 * W
        got = lax.dot_general(z3[0:span, :], b_ref[v * Q : (v + 1) * Q, :], CONTRACT_LANES, preferred_element_type=F32)
        for u in range(3):
            yield u * 3 + v, got[u * W : (u + 1) * W]
        if bias and v == 1:
            yield 9, got[3 * W :]


def interior_taps(tmp, b_ref, z3):
    zero = jnp.zeros((W, LANES), BF16)
    z3[0:W, 0:LANES] = zero
    z3[2 * W : 3 * W, CELLS - LANES :] = zero
    for r in range(ROWS):
        row = tmp[pl.ds(r, W, stride=ROWS), :].astype(BF16)
        for u in range(3):
            n = r + 1 - u
            if 0 <= n < ROWS:
                z3[u * W : (u + 1) * W, n * LANES : (n + 1) * LANES] = row
    ids = lax.broadcasted_iota(jnp.int32, (16, CELLS), 0)
    z3[3 * W :, :] = jnp.where(ids == 0, 1.0, 0.0).astype(BF16)
    yield from taps(z3, b_ref, True)


def halo_taps(tmp, b_ref, zh):
    zero = jnp.zeros((W, LANES), BF16)
    zh[0:W, 0:LANES] = zero
    zh[W : 2 * W, 0:LANES] = zero
    zh[2 * W :, 0:LANES] = tmp[pl.ds(0, W, stride=ROWS), :].astype(BF16)
    zh[0:W, LANES : 2 * LANES] = tmp[pl.ds(ROWS - 1, W, stride=ROWS), :].astype(BF16)
    zh[W : 2 * W, LANES : 2 * LANES] = zero
    zh[2 * W :, LANES : 2 * LANES] = zero
    step = 32
    lanes = lane_ids(step)
    half = LANES // 2
    for k in range(W // step):
        side = jnp.zeros((step, LANES), F32)
        for r in range(ROWS):
            row = tmp[pl.ds(k * step * ROWS + r, step, stride=ROWS), :]
            side = jnp.where(lanes == r, pltpu.roll(row, r + 1, 1), side)
            side = jnp.where(lanes == half + r, pltpu.roll(row, half + r, 1), side)
        for u in range(3):
            zh[pl.ds(u * W + k * step, step), 2 * LANES :] = (side if u == 2 else pltpu.roll(side, 2 - u, 1)).astype(BF16)
    yield from taps(zh, b_ref, False)


def accumulate_kernel(t, has_acc, with_halo, *refs):
    refs = list(refs)
    acc_ref = refs.pop(0) if has_acc else None
    x_ref, h_ref, b_ref = refs[:3]
    out_ref, z3, zh, tmp = refs[-4:]
    stack_fields(t, x_ref, h_ref, tmp)
    for tap, got in interior_taps(tmp, b_ref, z3):
        rows = slice(tap * W, tap * W + got.shape[0])
        out_ref[rows, :] = acc_ref[rows, :] + got if has_acc else got
    if with_halo:
        for tap, got in halo_taps(tmp, refs[3], zh):
            rows = slice(tap * W, tap * W + got.shape[0])
            out_ref[rows, :] += got


def z_windows(tmp, r0_ref, r1_ref, k0_ref, k1_ref, zw):
    step = 32
    lanes = lane_ids(step)
    for k in range(W // step):
        above, below = halo_rows(r0_ref, r1_ref, pl.ds(Q + k * step, step))
        left, right = halo_columns(k0_ref, k1_ref, pl.ds(k * step, step))
        left, right = corner_lanes(lanes, r0_ref, r1_ref, Q // step + k, left, right, ZLANE)
        for source in range(-1, ROWS + 1):
            if source < 0:
                row = above
            elif source == ROWS:
                row = below
            else:
                row = tmp[pl.ds(k * step * ROWS + source, step, stride=ROWS), :]
            lane = ZLANE + source + 1
            shifted = (
                jnp.where(lanes == 0, pltpu.roll(left, LANES - lane, 1), pltpu.roll(row, 1, 1)),
                row,
                jnp.where(lanes == LANES - 1, pltpu.roll(right, LANES - 1 - lane, 1), pltpu.roll(row, LANES - 1, 1)),
            )
            for v in range(3):
                block = shifted[v].astype(BF16)
                for u in range(3):
                    r = source - (u - 1)
                    if 0 <= r < ROWS:
                        zw[pl.ds((3 * u + v) * W + k * step, step), r * LANES : (r + 1) * LANES] = block
    ids = lax.broadcasted_iota(jnp.int32, (16, CELLS), 0)
    zw[9 * W :, :] = jnp.where(ids == 0, 1.0, 0.0).astype(BF16)


def send_kernel(blocks, scale, acc_ref, x_ref, h2_ref, b_ref, h_ref, r0_ref, r1_ref, k0_ref, k1_ref, a_ref, out_ref, zh, zw, tmp, total):
    stack_fields(0, x_ref, h_ref, tmp)
    z_windows(tmp, r0_ref, r1_ref, k0_ref, k1_ref, zw)
    total[...] = acc_ref[...] + lax.dot_general(zw[...], a_ref[...], CONTRACT_LANES, preferred_element_type=F32)
    stack_fields(1, x_ref, h2_ref, tmp)
    for tap, got in halo_taps(tmp, b_ref, zh):
        rows = slice(tap * W, tap * W + got.shape[0])
        total[rows, :] += got
    bias = total[9 * W : 9 * W + 8, :] * scale
    high = jnp.broadcast_to(bias[0:1], (8, Q)).astype(BF16).astype(F32)
    low = jnp.broadcast_to(bias[0:1], (8, Q)) - high
    ids = lax.broadcasted_iota(jnp.int32, (8, Q), 0)
    tail = jnp.where(ids == 0, high, jnp.where(ids == 1, low, 0.0))
    size = 9 * W // blocks
    for c in range(blocks):
        body = jnp.concatenate([total[c * size : (c + 1) * size, :] * scale, tail], axis=0)
        out_ref[c * (size + 8) : (c + 1) * (size + 8), :] = body.astype(BF16)


def result_kernel(blocks, in_ref, k_ref, bias_ref, scr):
    size = in_ref.shape[0] // blocks
    total = in_ref[0:size, :]
    for c in range(1, blocks):
        total = total + in_ref[c * size : (c + 1) * size, :]
    taps_here = k_ref.shape[1]
    k_ref[...] = total[:, 0:taps_here]
    scr[...] = jnp.broadcast_to(total[:, taps_here : taps_here + 1] + total[:, taps_here + 1 : taps_here + 2], scr.shape)
    count = bias_ref.shape[0]
    bias_ref[...] = scr[pl.ds(lax.axis_index("col") * count, count), 0:1]


def fold_kernel(blocks, in_ref, out_ref):
    size = in_ref.shape[0] // blocks
    total = in_ref[0:size, :].astype(F32)
    for c in range(1, blocks):
        total = total + in_ref[c * size : (c + 1) * size, :].astype(F32)
    out_ref[...] = total.T


def even_swap(count):
    return [(i, i ^ 1) for i in range(count)]


def odd_swap(count):
    return [(i, (i + 1) % count if i % 2 else (i - 1) % count) for i in range(count)]


def swaps(first, second, axis):
    count = lax.axis_size(axis)
    return lax.ppermute(first, axis, even_swap(count)), lax.ppermute(second, axis, odd_swap(count))


def struct(shape, dtype):
    return jax.ShapeDtypeStruct(shape, dtype)


def shards(inputs, gate_pre, cotangent, hidden_init, cell_init, land_mask, kernel):
    field = (CH, ROWS, LANES)
    nrow, ncol = lax.axis_size("row"), lax.axis_size("col")
    scale = 1.0 / math.sqrt(ROWS * LANES * nrow * ncol)
    edge = struct((Q, LANES), BF16)
    grads_out = (struct((Q, CELLS), BF16), edge, edge)
    scr = pltpu.VMEM((Q * ROWS, LANES), F32)
    y3 = pltpu.VMEM((3 * W, 3 * LANES), F32)
    tmp = pltpu.VMEM((W * ROWS, LANES), F32)
    z3, zh = pltpu.VMEM((ZROWS, CELLS), BF16), pltpu.VMEM((3 * W, 3 * LANES), BF16)
    hbm = pl.BlockSpec(memory_space=pltpu.MemorySpace.HBM)

    c1, c2, dc, a, p0, p1 = call(
        forward_kernel,
        (struct(field, F32), struct(field, F32), struct(field, F32)) + grads_out,
        in_specs=[hbm] * 4,
        out_specs=[whole()] * 6,
        scratch=[
            scr,
            pltpu.VMEM((3, Q, ROWS, LANES), BF16),
            pltpu.VMEM(field, BF16),
            pltpu.VMEM(field, F32),
            pltpu.VMEM((ROWS, LANES), jnp.int32),
            pltpu.SemaphoreType.DMA((13,)),
        ],
    )(*(in_hbm(x) for x in (gate_pre, cotangent, cell_init, land_mask)))

    h1, h2 = call(hidden_kernel, (struct(field, BF16),) * 2, in_specs=[whole()] * 4, out_specs=[whole()] * 2)(gate_pre, c1, c2, land_mask)
    cells = [cell_init, c1, c2]
    hiddens = [hidden_init, h1, h2]
    interior, halo = struct((3 * Q, CELLS), BF16), struct((3 * Q, 3 * LANES), BF16)
    acc_shape = struct((9 * W + 16, Q), F32)

    def corner(wide, r0, r1, ql, qr):
        out = call(functools.partial(corner_kernel, wide), (edge, edge), in_specs=[whole()] * 4, out_specs=[whole()] * 2)
        return out(r0, r1, ql, qr)

    def inside(a):
        return call(
            interior_kernel,
            (interior, struct((W, CELLS), F32)),
            in_specs=[whole()] * 2,
            out_specs=[whole()] * 2,
            scratch=[pltpu.VMEM((3 * W, CELLS), F32)],
        )(a, weights)

    def accumulate(t, acc, b, bh):
        head = [] if acc is None else [acc]
        rest = [b] if bh is None else [b, bh]
        return call(
            functools.partial(accumulate_kernel, t, acc is not None, bh is not None),
            acc_shape,
            in_specs=[whole()] * (len(head) + 2 + len(rest)),
            out_specs=whole(),
            scratch=[z3, zh, tmp],
            aliases={0: 0} if head else {},
        )(*head, inputs, hiddens[t], *rest)

    r0, r1 = swaps(p0, p1, "row")
    weights = call(weights_kernel, struct((3 * W, 3 * Q), BF16), in_specs=[whole()], out_specs=whole())(kernel)
    zedge = struct((W, LANES), BF16)
    z0, z1, ql, qr = call(
        edges_kernel,
        (zedge, zedge, edge, edge),
        in_specs=[whole()] * 8,
        out_specs=[whole()] * 4,
        scratch=[scr, pltpu.VMEM((3 * CH * ROWS, LANES), F32), tmp],
    )(a, gate_pre, cotangent, c1, dc, land_mask, inputs, hidden_init)
    r0, r1, weights, ql, qr = lax.optimization_barrier((r0, r1, weights, ql, qr))
    s0, s1 = corner(True, r0, r1, ql, qr)
    k0, k1 = swaps(s0, s1, "col")
    b, y = inside(a)
    pay = struct((CORNER + 32, LANES), BF16)
    gi2, bh, dc, a, p0, p1, pack = call(
        third_kernel,
        (struct(field, BF16), halo, struct(field, F32), struct((Q, CELLS), BF16), pay, pay, edge),
        in_specs=[whole()] * 16,
        out_specs=[whole()] * 7,
        scratch=[pltpu.VMEM((3 * Q, 4 * LANES), BF16), pltpu.VMEM((3 * W, 4 * LANES), F32), tmp, scr],
    )(r0, r1, k0, k1, s0, s1, z0, z1, weights, y, gate_pre, cotangent, cells[1], cells[2], land_mask, dc)
    r0, r1 = swaps(p0, p1, "row")
    acc = accumulate(2, None, b, bh)
    b, y = inside(a)
    acc = accumulate(1, acc, b, None)
    r0, r1, acc, y = lax.optimization_barrier((r0, r1, acc, y))
    gi1, bh, dc, a, p0, p1, ql, qr = call(
        second_kernel,
        (struct(field, BF16), halo, struct(field, F32)) + grads_out + (edge, edge),
        in_specs=[whole()] * 11,
        out_specs=[whole()] * 8,
        scratch=[y3, tmp, scr],
    )(r0, r1, pack, weights, y, gate_pre, cotangent, cells[0], cells[1], land_mask, dc)
    size = 9 * W // ncol + 8
    send = call(
        functools.partial(send_kernel, ncol, scale),
        struct((ncol * size, Q), BF16),
        in_specs=[whole()] * 10,
        out_specs=whole(),
        scratch=[zh, pltpu.VMEM((9 * W + 16, CELLS), BF16), tmp, pltpu.VMEM((9 * W + 16, Q), F32)],
    )(acc, inputs, hiddens[1], bh, hiddens[0], r0, r1, k0, k1, a)
    r0, r1 = swaps(p0, p1, "row")
    got = lax.all_to_all(send, "col", 0, 0, tiled=True)
    c0, c1 = corner(False, r0, r1, ql, qr)
    k0, k1 = swaps(c0, c1, "col")
    b, y = inside(a)
    got, c0, y = lax.optimization_barrier((got, c0, y))
    folded = call(functools.partial(fold_kernel, ncol), struct((Q, size), F32), in_specs=[whole()], out_specs=whole())(got)
    got = lax.all_to_all(folded, "row", 0, 0, tiled=True)
    y, folded = lax.optimization_barrier((y, folded))
    gi, grad_hidden, grad_cell = call(
        last_kernel,
        (struct((3,) + field, BF16), struct(field, F32), struct(field, F32)),
        in_specs=[whole()] * 9,
        out_specs=[whole()] * 3,
        scratch=[pltpu.VMEM((3 * Q, 3 * LANES), BF16), y3, tmp],
    )(gi1, gi2, dc, r0, r1, k0, k1, weights, y)
    count = Q // nrow // ncol
    grad_kernel, grad_bias = call(
        functools.partial(result_kernel, nrow),
        (struct((Q // nrow, size - 8), F32), struct((count, 1), F32)),
        in_specs=[whole()],
        out_specs=[whole()] * 2,
        scratch=[pltpu.VMEM((Q // nrow, LANES), F32)],
    )(got)
    return (gi, grad_hidden, grad_cell, grad_kernel, grad_bias.reshape(count))


def solution(mesh):
    placed = (
        P(None, None, "row", "col"),
        P(None, None, "row", "col"),
        P(None, None, "row", "col"),
        P(None, "row", "col"),
        P(None, "row", "col"),
        P("row", "col"),
        P(),
    )
    return jax.shard_map(
        shards,
        mesh=mesh,
        in_specs=placed,
        out_specs=(
            P(None, None, "row", "col"),
            P(None, "row", "col"),
            P(None, "row", "col"),
            P("row", "col"),
            P(("row", "col")),
        ),
        check_vma=False,
    )
```

```python
import functools
import math

import jax
import jax.numpy as jnp
from jax import lax
from jax.experimental import pallas as pl
from jax.experimental.pallas import tpu as pltpu
from jax.sharding import PartitionSpec as P


INTERPRET = False
VMEM_LIMIT = 24 << 20
F32 = jnp.float32
BF16 = jnp.bfloat16
ROWS = 8
LANES = 128
SLABS = ROWS + 2
CH = 64
Q = 4 * CH
W = 2 * CH


def call(body, out_shape, in_specs=None, out_specs=None, scratch=(), aliases=None):
    kwargs = {}
    if in_specs is not None:
        kwargs["in_specs"] = in_specs
    if out_specs is not None:
        kwargs["out_specs"] = out_specs
    return pl.pallas_call(
        body,
        out_shape=out_shape,
        scratch_shapes=list(scratch),
        input_output_aliases=aliases or {},
        interpret=INTERPRET,
        grid=(1,),
        compiler_params=pltpu.CompilerParams(vmem_limit_bytes=VMEM_LIMIT),
        **kwargs,
    )


def whole():
    return pl.BlockSpec(memory_space=pltpu.VMEM)


def in_hbm(x):
    return x if INTERPRET else pltpu.with_memory_space_constraint(x, pltpu.MemorySpace.HBM)


def sigmoid(x):
    return 0.5 * jnp.tanh(0.5 * x) + 0.5


def lane_ids(rows):
    return lax.broadcasted_iota(jnp.int32, (rows, LANES), 1)


def parity(axis):
    return lax.rem(lax.axis_index(axis), 2)


def edge_flags(axis):
    index = lax.axis_index(axis)
    low = jnp.where(index > 0, 1.0, 0.0).astype(F32)
    high = jnp.where(index < lax.axis_size(axis) - 1, 1.0, 0.0).astype(F32)
    return low, high


def gate_grads(pre, part, cot, dh, mask, cell_before, tanh_cell, dc):
    gin, gfor, gout, gcand = pre
    error = mask * (cot if dh is None else dh + cot)
    eo = error * gout
    grad = eo * (1.0 - tanh_cell * tanh_cell)
    if dc is not None:
        grad = dc + grad
    gi = grad * gin
    part[0] = gi * gcand * (1.0 - gin)
    df = grad * gfor
    part[1] = df * cell_before * (1.0 - gfor)
    part[2] = eo * tanh_cell * (1.0 - gout)
    part[3] = gi * (1.0 - gcand * gcand)
    return df


def by_parity(par, top, bottom, p0_ref, p1_ref, start):
    rows = slice(start, start + top.shape[0])

    @pl.when(par == 0)
    def _():
        p0_ref[rows, :] = bottom
        p1_ref[rows, :] = top

    @pl.when(par == 1)
    def _():
        p0_ref[rows, :] = top
        p1_ref[rows, :] = bottom


def emit_grads(scr, a_ref, p0_ref, p1_ref, packs=None):
    step = 32
    lanes = lane_ids(step)
    for k in range(Q // step):
        own = pl.ds(k * step, step)
        ql = jnp.zeros((step, LANES), F32)
        qr = jnp.zeros((step, LANES), F32)
        for r in range(ROWS):
            row = scr[pl.ds(k * step * ROWS + r, step, stride=ROWS), :]
            a_ref[own, r * LANES : (r + 1) * LANES] = row.astype(BF16)
            if packs:
                ql = jnp.where(lanes == r + 1, pltpu.roll(row, r + 1, 1), ql)
                qr = jnp.where(lanes == r + 1, pltpu.roll(row, r + 2, 1), qr)
        if packs:
            packs[0][own, :] = ql.astype(BF16)
            packs[1][own, :] = qr.astype(BF16)
    by_parity(parity("row"), a_ref[:, 0:LANES], a_ref[:, (ROWS - 1) * LANES :], p0_ref, p1_ref, 0)


def forward_kernel(pre_hbm, cot_hbm, c0_hbm, mask_hbm, h0_hbm, k_hbm, c1_ref, c2_ref, dc_ref, a_ref, p0_ref, p1_ref, c0_ref, mask_ref, h0_ref, k_ref, scr, pre_ref, cot_ref, sems):
    pairs = [(c0_hbm, c0_ref), (mask_hbm, mask_ref), (cot_hbm.at[2], cot_ref)]
    for t, g in ((0, 1), (0, 0), (0, 3), (1, 1), (1, 0), (1, 3), (2, 1), (2, 0), (2, 3), (2, 2)):
        own = pl.ds(g * CH, CH)
        pairs.append((pre_hbm.at[t, own], pre_ref.at[t, own]))
    copies = [pltpu.make_async_copy(src, dst, sems.at[n]) for n, (src, dst) in enumerate(pairs)]
    order = [3, 4, 0, 5, 6, 7, 8, 9, 10, 11, 12, 2, 1]
    for n in order:
        copies[n].start()
    later = [pltpu.make_async_copy(src, dst, sems.at[13 + n]) for n, (src, dst) in enumerate(((k_hbm, k_ref), (h0_hbm, h0_ref)))]
    for copy in later:
        copy.start()
    step = 8

    def gate(t, g, base):
        return pre_ref[t, pl.ds(g * CH + base, step)].astype(F32)

    copies[0].wait()
    for t, (before_ref, c_ref) in enumerate(((c0_ref, c1_ref), (c1_ref, c2_ref))):
        for n in range(3 + 3 * t, 6 + 3 * t):
            copies[n].wait()

        def advance(j, carry):
            base = j * step
            own = pl.ds(base, step)
            c_ref[own] = sigmoid(gate(t, 1, base)) * before_ref[own] + sigmoid(gate(t, 0, base)) * jnp.tanh(gate(t, 3, base))
            return carry

        lax.fori_loop(0, CH // step, advance, 0)
    for n in (9, 10, 11, 12, 2, 1):
        copies[n].wait()
    mask = mask_ref[...].astype(F32)[None]

    def chunk(j, carry):
        base = j * step
        own = pl.ds(base, step)
        cell = c2_ref[own]
        pre = (sigmoid(gate(2, 0, base)), sigmoid(gate(2, 1, base)), sigmoid(gate(2, 2, base)), jnp.tanh(gate(2, 3, base)))
        tanh_cell = jnp.tanh(pre[1] * cell + pre[0] * pre[3])
        part = [None] * 4
        dc_ref[own] = gate_grads(pre, part, cot_ref[own].astype(F32), None, mask, cell, tanh_cell, None)
        for g in range(4):
            scr[pl.ds((g * CH + base) * ROWS, step * ROWS), :] = part[g].reshape(step * ROWS, LANES)
        return carry

    lax.fori_loop(0, CH // step, chunk, 0)
    emit_grads(scr, a_ref, p0_ref, p1_ref)
    for copy in later:
        copy.wait()


def hidden_kernel(pre_ref, c1_ref, c2_ref, mask_ref, h1_ref, h2_ref):
    step = 8
    mask = mask_ref[...].astype(F32)[None]
    for t, (c_ref, h_ref) in enumerate(((c1_ref, h1_ref), (c2_ref, h2_ref))):

        def chunk(j, carry):
            own = pl.ds(j * step, step)
            gout = sigmoid(pre_ref[t, pl.ds(2 * CH + j * step, step)].astype(F32))
            h_ref[own] = (mask * gout * jnp.tanh(c_ref[own])).astype(BF16)
            return carry

        lax.fori_loop(0, CH // step, chunk, 0)


def weights_kernel(k_ref, w_ref):
    for u in range(3):
        for v in range(3):
            tap = (3 * u + v) * W
            w_ref[u * W : (u + 1) * W, v * Q : (v + 1) * Q] = k_ref[:, tap : tap + W].astype(F32).T.astype(BF16)


def halo_rows(r0_ref, r1_ref, own):
    par = parity("row").astype(F32)
    low, high = edge_flags("row")
    first, second = r0_ref[own, :].astype(F32), r1_ref[own, :].astype(F32)
    above = second * ((1.0 - par) * low) + first * (par * low)
    below = first * ((1.0 - par) * high) + second * (par * high)
    return above, below


SECOND, PRE, STATE, ZLANE = 16, 32, 48, 64
CORNER = Q + W


def move(x, source, target):
    shift = (target - source) % LANES
    return pltpu.roll(x, shift, 1) if shift else x


def corner_kernel(wide, r0_ref, r1_ref, ql_ref, qr_ref, c0_ref, c1_ref):
    par = parity("col").astype(F32)
    step = 32
    lanes = lane_ids(step)
    for k in range(Q // step):
        own = pl.ds(k * step, step)
        above, below = halo_rows(r0_ref, r1_ref, own)
        left, right = ql_ref[own, :].astype(F32), qr_ref[own, :].astype(F32)
        for depth in range(2 if wide else 1):
            for row, lane in ((above, depth * SECOND), (below, depth * SECOND + SLABS - 1)):
                left = jnp.where(lanes == lane, move(row, depth, lane), left)
                right = jnp.where(lanes == lane, move(row, LANES - 1 - depth, lane), right)
        c0_ref[own, :] = (right * (1.0 - par) + left * par).astype(BF16)
        c1_ref[own, :] = (left * (1.0 - par) + right * par).astype(BF16)


def halo_columns(c0_ref, c1_ref, own):
    par = parity("col").astype(F32)
    low, high = edge_flags("col")
    first, second = c0_ref[own, :].astype(F32), c1_ref[own, :].astype(F32)
    left = second * ((1.0 - par) * low) + first * (par * low)
    right = first * ((1.0 - par) * high) + second * (par * high)
    return left, right


def edges_kernel(a_ref, pre_ref, cot_ref, cell_ref, dc_ref, mask_ref, x_ref, h_ref, p0_ref, p1_ref, ql_ref, qr_ref, pre_tmp, state, tmp):
    stack_fields(0, x_ref, h_ref, tmp)
    top = tmp[pl.ds(0, W, stride=ROWS), :].astype(BF16)
    bottom = tmp[pl.ds(ROWS - 1, W, stride=ROWS), :].astype(BF16)
    by_parity(parity("row"), top, bottom, p0_ref, p1_ref, 0)
    land = mask_ref[...][None] > 0
    size = CH * ROWS
    for g in range(4):
        block = pre_ref[1, g * CH : (g + 1) * CH].astype(F32)
        if g == 2:
            block = jnp.where(land, block, -64.0)
        pre_tmp[g * size : (g + 1) * size, :] = block.reshape(size, LANES)
    state[0:size, :] = cot_ref[1].astype(F32).reshape(size, LANES)
    state[size : 2 * size, :] = cell_ref[...].reshape(size, LANES)
    state[2 * size :, :] = dc_ref[...].reshape(size, LANES)
    step = 32
    lanes = lane_ids(step)
    for k in range(Q // step):
        left = jnp.zeros((step, LANES), F32)
        right = jnp.zeros((step, LANES), F32)
        for r in range(ROWS):
            own = pl.ds(k * step * ROWS + r, step, stride=ROWS)
            row = a_ref[pl.ds(k * step, step), r * LANES : (r + 1) * LANES].astype(F32)
            pieces = [(row, 0, 0), (row, 1, SECOND), (pre_tmp[own, :], 0, PRE)]
            if k < 3 * CH // step:
                pieces.append((state[own, :], 0, STATE))
            if k < W // step:
                pieces.append((tmp[own, :], 0, ZLANE))
            for piece, depth, slot in pieces:
                lane = slot + r + 1
                left = jnp.where(lanes == lane, move(piece, depth, lane), left)
                right = jnp.where(lanes == lane, move(piece, LANES - 1 - depth, lane), right)
        ql_ref[pl.ds(k * step, step), :] = left.astype(BF16)
        qr_ref[pl.ds(k * step, step), :] = right.astype(BF16)


def interior_kernel(a_ref, w_ref, b_ref, y_ref, y3):
    step = 32
    lanes = lane_ids(step)
    for k in range(Q // step):
        for r in range(ROWS):
            span = slice(r * LANES, (r + 1) * LANES)
            block = a_ref[pl.ds(k * step, step), span]
            row = block.astype(F32)
            minus = jnp.where(lanes == LANES - 1, 0.0, pltpu.roll(row, LANES - 1, 1))
            plus = jnp.where(lanes == 0, 0.0, pltpu.roll(row, 1, 1))
            b_ref[pl.ds(k * step, step), span] = minus.astype(BF16)
            b_ref[pl.ds(Q + k * step, step), span] = block
            b_ref[pl.ds(2 * Q + k * step, step), span] = plus.astype(BF16)
    y3[...] = lax.dot_general(w_ref[...], b_ref[...], (((1,), (0,)), ((), ())), preferred_element_type=F32)
    for r in range(ROWS):
        total = y3[W : 2 * W, r * LANES : (r + 1) * LANES]
        if r < ROWS - 1:
            total = total + y3[0:W, (r + 1) * LANES : (r + 2) * LANES]
        if r > 0:
            total = total + y3[2 * W : 3 * W, (r - 1) * LANES : r * LANES]
        y_ref[:, r * LANES : (r + 1) * LANES] = total


def travelled(r0_ref, r1_ref, c0_ref, c1_ref):
    def source(k, step):
        own = pl.ds(k * step, step)
        return halo_rows(r0_ref, r1_ref, own) + halo_columns(c0_ref, c1_ref, own)

    return source


def corner_lanes(lanes, r0_ref, r1_ref, group, left, right, first):
    above, below = halo_rows(r0_ref, r1_ref, pl.ds(CORNER, 32))
    for row, lane in ((above, first), (below, first + SLABS - 1)):
        right = jnp.where(lanes == lane, move(row, 2 * group, lane), right)
        left = jnp.where(lanes == lane, move(row, 2 * group + 1, lane), left)
    return left, right


def computed(r0_ref, r1_ref, pack_ref):
    def source(k, step):
        own = pl.ds(k * step, step)
        pack = pack_ref[own, :].astype(F32)
        columns = corner_lanes(lane_ids(step), r0_ref, r1_ref, k, pltpu.roll(pack, LANES // 2, 1), pack, 0)
        return halo_rows(r0_ref, r1_ref, own) + columns

    return source


def build_halo(source, b_ref):
    step = 32
    lanes = lane_ids(step)
    inside = (lanes >= 1) & (lanes <= ROWS)
    last = SLABS - 1
    for k in range(Q // step):
        above, below, left, right = source(k, step)
        for n, (row, s) in enumerate(((above, 0), (below, last))):
            span = slice(n * LANES, (n + 1) * LANES)
            minus = jnp.where(lanes == LANES - 1, pltpu.roll(right, LANES - 1 - s, 1), pltpu.roll(row, LANES - 1, 1))
            plus = jnp.where(lanes == 0, pltpu.roll(left, (LANES - s) % LANES, 1), pltpu.roll(row, 1, 1))
            b_ref[pl.ds(k * step, step), span] = minus.astype(BF16)
            b_ref[pl.ds(Q + k * step, step), span] = row.astype(BF16)
            b_ref[pl.ds(2 * Q + k * step, step), span] = plus.astype(BF16)
        span = slice(2 * LANES, 3 * LANES)
        b_ref[pl.ds(k * step, step), span] = jnp.where(inside, right, 0.0).astype(BF16)
        b_ref[pl.ds(Q + k * step, step), span] = jnp.zeros((step, LANES), BF16)
        b_ref[pl.ds(2 * Q + k * step, step), span] = pltpu.roll(jnp.where(inside, left, 0.0), LANES // 2, 1).astype(BF16)


def finish_y(w_ref, b_ref, y_ref, y3, scr):
    y3[...] = lax.dot_general(w_ref[...], b_ref[...], (((1,), (0,)), ((), ())), preferred_element_type=F32)
    step = 32
    lanes = lane_ids(step)
    for k in range(W // step):
        side = 0.0
        for u in range(3):
            piece = y3[pl.ds(u * W + k * step, step), 2 * LANES : 3 * LANES]
            side = side + (piece if u == 2 else pltpu.roll(piece, LANES + u - 2, 1))
        for r in range(ROWS):
            total = y_ref[pl.ds(k * step, step), r * LANES : (r + 1) * LANES]
            if r == 0:
                total = total + y3[pl.ds(2 * W + k * step, step), 0:LANES]
            if r == ROWS - 1:
                total = total + y3[pl.ds(k * step, step), LANES : 2 * LANES]
            right = jnp.where(lanes == LANES - 1, pltpu.roll(side, LANES - 1 - r, 1), 0.0)
            left = jnp.where(lanes == 0, pltpu.roll(side, LANES // 2 - r, 1), right)
            scr[pl.ds(k * step * ROWS + r, step, stride=ROWS), :] = total + left


def factors_kernel(t, pre_ref, cot_ref, before_ref, cell_ref, mask_ref, *out_refs):
    step = 8
    mask = mask_ref[...].astype(F32)[None]

    def chunk(j, carry):
        base = j * step
        own = pl.ds(base, step)

        def gate(g):
            return pre_ref[t, pl.ds(g * CH + base, step)].astype(F32)

        gin, gfor, gout, gcand = sigmoid(gate(0)), sigmoid(gate(1)), sigmoid(gate(2)), jnp.tanh(gate(3))
        tanh_cell = jnp.tanh(cell_ref[own])
        open_mask = mask * gout
        values = (
            open_mask,
            open_mask * cot_ref[t, own].astype(F32),
            1.0 - tanh_cell * tanh_cell,
            gcand * gin * (1.0 - gin),
            before_ref[own] * gfor * (1.0 - gfor),
            tanh_cell * (1.0 - gout),
            gin * (1.0 - gcand * gcand),
            gfor,
        )
        for ref, value in zip(out_refs, values):
            ref[own] = value
        return carry

    lax.fori_loop(0, CH // step, chunk, 0)


def step_grads(factors, dc_in, gi_ref, dc_ref, yscr, scr):
    step = 8
    open_ref, cot_ref, slope_ref, in_ref, for_ref, out_ref, cand_ref, keep_ref = factors

    def chunk(j, carry):
        base = j * step
        own = pl.ds(base, step)
        gi_ref[own] = yscr[pl.ds(base * ROWS, step * ROWS), :].reshape(step, ROWS, LANES).astype(BF16)
        dh = yscr[pl.ds((CH + base) * ROWS, step * ROWS), :].reshape(step, ROWS, LANES)
        error = dh * open_ref[own] + cot_ref[own]
        grad = dc_in[own] + error * slope_ref[own]
        part = (grad * in_ref[own], grad * for_ref[own], error * out_ref[own], grad * cand_ref[own])
        dc_ref[own] = grad * keep_ref[own]
        for g in range(4):
            scr[pl.ds((g * CH + base) * ROWS, step * ROWS), :] = part[g].reshape(step * ROWS, LANES)
        return carry

    lax.fori_loop(0, CH // step, chunk, 0)


def third_kernel(*refs):
    factors, refs = refs[:8], refs[8:]
    (r0_ref, r1_ref, k0_ref, k1_ref, s0_ref, s1_ref, z0_ref, z1_ref, w_ref, y_ref, dc_in,
     gi_ref, bh_ref, dc_ref, a_ref, p0_ref, p1_ref, pack_ref, b_ref, y3, yscr, scr) = refs
    build_halo(travelled(r0_ref, r1_ref, k0_ref, k1_ref), b_ref)
    par = parity("col").astype(F32)
    step = 32
    half = LANES // 2
    lanes = lane_ids(step)
    first, second = lanes < SLABS, (lanes >= half) & (lanes < half + SLABS)
    for k in range(Q // step):
        own = pl.ds(k * step, step)
        left, right = halo_columns(k0_ref, k1_ref, own)
        sent0, sent1 = s0_ref[own, :].astype(F32), s1_ref[own, :].astype(F32)
        my_right = sent0 * (1.0 - par) + sent1 * par
        my_left = sent1 * (1.0 - par) + sent0 * par
        pairs = (
            (move(right, SECOND, 0), move(my_left, 0, half)),
            (right, move(left, 0, half)),
            (my_right, move(left, SECOND, half)),
        )
        for v, (low, high) in enumerate(pairs):
            b_ref[pl.ds(v * Q + k * step, step), 3 * LANES :] = jnp.where(first, low, jnp.where(second, high, 0.0)).astype(BF16)
    bh_ref[...] = b_ref[:, 0 : 3 * LANES]
    finish_y(w_ref, b_ref, y_ref, y3, yscr)
    step_grads(factors, dc_in, gi_ref, dc_ref, yscr, scr)
    low, high = edge_flags("col")
    valid = jnp.where((lanes >= 1) & (lanes <= ROWS), high, jnp.where((lanes > half) & (lanes <= half + ROWS), low, 0.0))
    for j in range(CH // step):

        def border(start, slot):
            left, right = halo_columns(k0_ref, k1_ref, pl.ds(start + j * step, step))
            return jnp.where(lanes < half, move(right, slot, 0), move(left, slot, half))

        dh = 0.0
        for u in range(3):
            dh = dh + move(y3[pl.ds(u * W + CH + j * step, step), 3 * LANES :], 1, u)
        gates = [border(g * CH, PRE) for g in range(4)]
        cot, before, dc = (border(m * CH, STATE) for m in range(3))
        pre = (sigmoid(gates[0]), sigmoid(gates[1]), sigmoid(gates[2]), jnp.tanh(gates[3]))
        tanh_cell = jnp.tanh(pre[1] * before + pre[0] * pre[3])
        part = [None] * 4
        gate_grads(pre, part, cot, dh, valid, before, tanh_cell, dc * valid)
        for g in range(4):
            pack_ref[pl.ds(g * CH + j * step, step), :] = part[g].astype(BF16)
    emit_grads(scr, a_ref, p0_ref, p1_ref)
    p0_ref[Q:CORNER, :] = z0_ref[...]
    p1_ref[Q:CORNER, :] = z1_ref[...]
    corners = []
    for r in (0, ROWS - 1):
        block = jnp.zeros((step, LANES), F32)
        for k in range(Q // step):
            pack = pack_ref[pl.ds(k * step, step), :].astype(F32)
            block = jnp.where(lanes == 2 * k, move(pack, r + 1, 2 * k), block)
            block = jnp.where(lanes == 2 * k + 1, move(pack, half + r + 1, 2 * k + 1), block)
        for k in range(W // step):
            left, right = halo_columns(k0_ref, k1_ref, pl.ds(k * step, step))
            lane = 2 * (Q // step + k)
            block = jnp.where(lanes == lane, move(right, ZLANE + r + 1, lane), block)
            block = jnp.where(lanes == lane + 1, move(left, ZLANE + r + 1, lane + 1), block)
        corners.append(block.astype(BF16))
    by_parity(parity("row"), corners[0], corners[1], p0_ref, p1_ref, CORNER)


def second_kernel(*refs):
    factors, refs = refs[:8], refs[8:]
    (r0_ref, r1_ref, pack_ref, w_ref, y_ref, dc_in,
     gi_ref, b_ref, dc_ref, a_ref, p0_ref, p1_ref, ql_ref, qr_ref, y3, yscr, scr) = refs
    build_halo(computed(r0_ref, r1_ref, pack_ref), b_ref)
    finish_y(w_ref, b_ref, y_ref, y3, yscr)
    step_grads(factors, dc_in, gi_ref, dc_ref, yscr, scr)
    emit_grads(scr, a_ref, p0_ref, p1_ref, (ql_ref, qr_ref))


def last_kernel(gi1_ref, gi2_ref, dc_ref, r0_ref, r1_ref, k0_ref, k1_ref, w_ref, y_ref, gi_ref, dh_ref, cell_ref, b_ref, y3, yscr):
    build_halo(travelled(r0_ref, r1_ref, k0_ref, k1_ref), b_ref)
    finish_y(w_ref, b_ref, y_ref, y3, yscr)
    gi_ref[0] = yscr[0 : CH * ROWS, :].reshape(CH, ROWS, LANES).astype(BF16)
    gi_ref[1] = gi1_ref[...]
    gi_ref[2] = gi2_ref[...]
    cell_ref[...] = dc_ref[...]
    dh_ref[...] = yscr[CH * ROWS :, :].reshape(CH, ROWS, LANES)


ZROWS = 3 * W + 16
CELLS = ROWS * LANES
CONTRACT_LANES = (((1,), (1,)), ((), ()))


def stack_fields(t, x_ref, h_ref, tmp):
    tmp[0 : CH * ROWS, :] = x_ref[t].astype(F32).reshape(CH * ROWS, LANES)
    tmp[CH * ROWS :, :] = h_ref[...].astype(F32).reshape(CH * ROWS, LANES)


def taps(z3, b_ref, bias):
    for v in range(3):
        span = ZROWS if bias and v == 1 else 3 * W
        got = lax.dot_general(z3[0:span, :], b_ref[v * Q : (v + 1) * Q, :], CONTRACT_LANES, preferred_element_type=F32)
        for u in range(3):
            yield u * 3 + v, got[u * W : (u + 1) * W]
        if bias and v == 1:
            yield 9, got[3 * W :]


def interior_taps(tmp, b_ref, z3):
    zero = jnp.zeros((W, LANES), BF16)
    z3[0:W, 0:LANES] = zero
    z3[2 * W : 3 * W, CELLS - LANES :] = zero
    for r in range(ROWS):
        row = tmp[pl.ds(r, W, stride=ROWS), :].astype(BF16)
        for u in range(3):
            n = r + 1 - u
            if 0 <= n < ROWS:
                z3[u * W : (u + 1) * W, n * LANES : (n + 1) * LANES] = row
    ids = lax.broadcasted_iota(jnp.int32, (16, CELLS), 0)
    z3[3 * W :, :] = jnp.where(ids == 0, 1.0, 0.0).astype(BF16)
    yield from taps(z3, b_ref, True)


def halo_taps(tmp, b_ref, zh):
    zero = jnp.zeros((W, LANES), BF16)
    zh[0:W, 0:LANES] = zero
    zh[W : 2 * W, 0:LANES] = zero
    zh[2 * W :, 0:LANES] = tmp[pl.ds(0, W, stride=ROWS), :].astype(BF16)
    zh[0:W, LANES : 2 * LANES] = tmp[pl.ds(ROWS - 1, W, stride=ROWS), :].astype(BF16)
    zh[W : 2 * W, LANES : 2 * LANES] = zero
    zh[2 * W :, LANES : 2 * LANES] = zero
    step = 32
    lanes = lane_ids(step)
    half = LANES // 2
    for k in range(W // step):
        side = jnp.zeros((step, LANES), F32)
        for r in range(ROWS):
            row = tmp[pl.ds(k * step * ROWS + r, step, stride=ROWS), :]
            side = jnp.where(lanes == r, pltpu.roll(row, r + 1, 1), side)
            side = jnp.where(lanes == half + r, pltpu.roll(row, half + r, 1), side)
        for u in range(3):
            zh[pl.ds(u * W + k * step, step), 2 * LANES :] = (side if u == 2 else pltpu.roll(side, 2 - u, 1)).astype(BF16)
    yield from taps(zh, b_ref, False)


def accumulate_kernel(t, has_acc, with_halo, *refs):
    refs = list(refs)
    acc_ref = refs.pop(0) if has_acc else None
    x_ref, h_ref, b_ref = refs[:3]
    out_ref, z3, zh, tmp = refs[-4:]
    stack_fields(t, x_ref, h_ref, tmp)
    for tap, got in interior_taps(tmp, b_ref, z3):
        rows = slice(tap * W, tap * W + got.shape[0])
        out_ref[rows, :] = acc_ref[rows, :] + got if has_acc else got
    if with_halo:
        for tap, got in halo_taps(tmp, refs[3], zh):
            rows = slice(tap * W, tap * W + got.shape[0])
            out_ref[rows, :] += got


def z_windows(tmp, r0_ref, r1_ref, k0_ref, k1_ref, zw):
    step = 32
    lanes = lane_ids(step)
    for k in range(W // step):
        above, below = halo_rows(r0_ref, r1_ref, pl.ds(Q + k * step, step))
        left, right = halo_columns(k0_ref, k1_ref, pl.ds(k * step, step))
        left, right = corner_lanes(lanes, r0_ref, r1_ref, Q // step + k, left, right, ZLANE)
        for source in range(-1, ROWS + 1):
            if source < 0:
                row = above
            elif source == ROWS:
                row = below
            else:
                row = tmp[pl.ds(k * step * ROWS + source, step, stride=ROWS), :]
            lane = ZLANE + source + 1
            shifted = (
                jnp.where(lanes == 0, pltpu.roll(left, LANES - lane, 1), pltpu.roll(row, 1, 1)),
                row,
                jnp.where(lanes == LANES - 1, pltpu.roll(right, LANES - 1 - lane, 1), pltpu.roll(row, LANES - 1, 1)),
            )
            for v in range(3):
                block = shifted[v].astype(BF16)
                for u in range(3):
                    r = source - (u - 1)
                    if 0 <= r < ROWS:
                        zw[pl.ds((3 * u + v) * W + k * step, step), r * LANES : (r + 1) * LANES] = block
    ids = lax.broadcasted_iota(jnp.int32, (16, CELLS), 0)
    zw[9 * W :, :] = jnp.where(ids == 0, 1.0, 0.0).astype(BF16)


def send_kernel(blocks, scale, acc_ref, x_ref, h2_ref, b_ref, h_ref, r0_ref, r1_ref, k0_ref, k1_ref, a_ref, out_hbm, zh, zw, tmp, total, stage, sems):
    stack_fields(1, x_ref, h2_ref, tmp)
    for tap, got in halo_taps(tmp, b_ref, zh):
        rows = slice(tap * W, tap * W + got.shape[0])
        total[rows, :] = acc_ref[rows, :] + got
    stack_fields(0, x_ref, h_ref, tmp)
    z_windows(tmp, r0_ref, r1_ref, k0_ref, k1_ref, zw)

    def product(rows):
        return lax.dot_general(zw[rows, :], a_ref[...], CONTRACT_LANES, preferred_element_type=F32)

    bias = (acc_ref[9 * W :, :] + product(slice(9 * W, 9 * W + 16)))[0:8] * scale
    high = jnp.broadcast_to(bias[0:1], (8, Q)).astype(BF16).astype(F32)
    low = jnp.broadcast_to(bias[0:1], (8, Q)) - high
    ids = lax.broadcasted_iota(jnp.int32, (8, Q), 0)
    tail = jnp.where(ids == 0, high, jnp.where(ids == 1, low, 0.0))
    size = 9 * W // blocks
    parts = sems.shape[0]
    each = blocks // parts
    copies = []
    for n in range(parts):
        rows = slice(n * each * size, (n + 1) * each * size)
        got = (total[rows, :] + product(rows)) * scale
        for c in range(each):
            start = (n * each + c) * (size + 8)
            stage[start : start + size + 8, :] = jnp.concatenate([got[c * size : (c + 1) * size], tail], axis=0).astype(BF16)
        span = pl.ds(n * each * (size + 8), each * (size + 8))
        copies.append(pltpu.make_async_copy(stage.at[span], out_hbm.at[span], sems.at[n]))
        copies[-1].start()
    for copy in copies:
        copy.wait()


def result_kernel(blocks, in_ref, k_ref, bias_ref, scr):
    size = in_ref.shape[0] // blocks
    total = in_ref[0:size, :]
    for c in range(1, blocks):
        total = total + in_ref[c * size : (c + 1) * size, :]
    taps_here = k_ref.shape[1]
    k_ref[...] = total[:, 0:taps_here]
    scr[...] = jnp.broadcast_to(total[:, taps_here : taps_here + 1] + total[:, taps_here + 1 : taps_here + 2], scr.shape)
    count = bias_ref.shape[0]
    bias_ref[...] = scr[pl.ds(lax.axis_index("col") * count, count), 0:1]


def fold_kernel(blocks, in_ref, out_ref):
    size = in_ref.shape[0] // blocks
    total = in_ref[0:size, :].astype(F32)
    for c in range(1, blocks):
        total = total + in_ref[c * size : (c + 1) * size, :].astype(F32)
    out_ref[...] = total.T


def even_swap(count):
    return [(i, i ^ 1) for i in range(count)]


def odd_swap(count):
    return [(i, (i + 1) % count if i % 2 else (i - 1) % count) for i in range(count)]


def swaps(first, second, axis):
    count = lax.axis_size(axis)
    first = lax.ppermute(first, axis, even_swap(count))
    second = lax.ppermute(second, axis, odd_swap(count))
    return first, second


def struct(shape, dtype):
    return jax.ShapeDtypeStruct(shape, dtype)


def shards(inputs, gate_pre, cotangent, hidden_init, cell_init, land_mask, kernel):
    field = (CH, ROWS, LANES)
    nrow, ncol = lax.axis_size("row"), lax.axis_size("col")
    scale = 1.0 / math.sqrt(ROWS * LANES * nrow * ncol)
    edge = struct((Q, LANES), BF16)
    grads_out = (struct((Q, CELLS), BF16), edge, edge)
    scr = pltpu.VMEM((Q * ROWS, LANES), F32)
    y3 = pltpu.VMEM((3 * W, 3 * LANES), F32)
    tmp = pltpu.VMEM((W * ROWS, LANES), F32)
    z3, zh = pltpu.VMEM((ZROWS, CELLS), BF16), pltpu.VMEM((3 * W, 3 * LANES), BF16)
    hbm = pl.BlockSpec(memory_space=pltpu.MemorySpace.HBM)

    c1, c2, dc, a, p0, p1, cell_init, land_mask, hidden_init, kernel = call(
        forward_kernel,
        (struct(field, F32), struct(field, F32), struct(field, F32))
        + grads_out
        + (struct(field, F32), struct((ROWS, LANES), jnp.int32), struct(field, BF16), struct(kernel.shape, BF16)),
        in_specs=[hbm] * 6,
        out_specs=[whole()] * 10,
        scratch=[
            scr,
            pltpu.VMEM((3, Q, ROWS, LANES), BF16),
            pltpu.VMEM(field, BF16),
            pltpu.SemaphoreType.DMA((15,)),
        ],
    )(*(in_hbm(x) for x in (gate_pre, cotangent, cell_init, land_mask, hidden_init, kernel)))

    h1, h2 = call(hidden_kernel, (struct(field, BF16),) * 2, in_specs=[whole()] * 4, out_specs=[whole()] * 2)(gate_pre, c1, c2, land_mask)
    cells = [cell_init, c1, c2]
    interior, halo = struct((3 * Q, CELLS), BF16), struct((3 * Q, 3 * LANES), BF16)
    acc_shape = struct((9 * W + 16, Q), F32)

    def corner(wide, r0, r1, ql, qr):
        out = call(functools.partial(corner_kernel, wide), (edge, edge), in_specs=[whole()] * 4, out_specs=[whole()] * 2)
        return out(r0, r1, ql, qr)

    def inside(a):
        return call(
            interior_kernel,
            (interior, struct((W, CELLS), F32)),
            in_specs=[whole()] * 2,
            out_specs=[whole()] * 2,
            scratch=[pltpu.VMEM((3 * W, CELLS), F32)],
        )(a, weights)

    def accumulate(t, acc, b, bh):
        head = [] if acc is None else [acc]
        rest = [b] if bh is None else [b, bh]
        return call(
            functools.partial(accumulate_kernel, t, acc is not None, bh is not None),
            acc_shape,
            in_specs=[whole()] * (len(head) + 2 + len(rest)),
            out_specs=whole(),
            scratch=[z3, zh, tmp],
            aliases={0: 0} if head else {},
        )(*head, inputs, hiddens[t], *rest)

    r0, r1 = swaps(p0, p1, "row")
    weights = call(weights_kernel, struct((3 * W, 3 * Q), BF16), in_specs=[whole()], out_specs=whole())(kernel)
    zedge = struct((W, LANES), BF16)
    z0, z1, ql, qr = call(
        edges_kernel,
        (zedge, zedge, edge, edge),
        in_specs=[whole()] * 8,
        out_specs=[whole()] * 4,
        scratch=[scr, pltpu.VMEM((3 * CH * ROWS, LANES), F32), tmp],
    )(a, gate_pre, cotangent, c1, dc, land_mask, inputs, hidden_init)
    r0, r1, weights, ql, qr = lax.optimization_barrier((r0, r1, weights, ql, qr))
    hiddens = [hidden_init, h1, h2]
    s0, s1 = corner(True, r0, r1, ql, qr)
    k0, k1 = swaps(s0, s1, "col")
    b, y = inside(a)
    earlier, later = (
        call(
            functools.partial(factors_kernel, t),
            (struct(field, F32),) * 8,
            in_specs=[whole()] * 5,
            out_specs=[whole()] * 8,
        )(gate_pre, cotangent, cells[t], cells[t + 1], land_mask)
        for t in range(2)
    )
    k0, k1, earlier, later = lax.optimization_barrier((k0, k1, earlier, later))
    pay = struct((CORNER + 32, LANES), BF16)
    gi2, bh, dc, a, p0, p1, pack = call(
        third_kernel,
        (struct(field, BF16), halo, struct(field, F32), struct((Q, CELLS), BF16), pay, pay, edge),
        in_specs=[whole()] * 19,
        out_specs=[whole()] * 7,
        scratch=[pltpu.VMEM((3 * Q, 4 * LANES), BF16), pltpu.VMEM((3 * W, 4 * LANES), F32), tmp, scr],
    )(*later, r0, r1, k0, k1, s0, s1, z0, z1, weights, y, dc)
    r0, r1 = swaps(p0, p1, "row")
    acc = accumulate(2, None, b, bh)
    b, y = inside(a)
    acc = accumulate(1, acc, b, None)
    r0, r1, acc, y = lax.optimization_barrier((r0, r1, acc, y))
    gi1, bh, dc, a, p0, p1, ql, qr = call(
        second_kernel,
        (struct(field, BF16), halo, struct(field, F32)) + grads_out + (edge, edge),
        in_specs=[whole()] * 14,
        out_specs=[whole()] * 8,
        scratch=[y3, tmp, scr],
    )(*earlier, r0, r1, pack, weights, y, dc)
    size = 9 * W // ncol + 8
    send = call(
        functools.partial(send_kernel, ncol, scale),
        struct((ncol * size, Q), BF16),
        in_specs=[whole()] * 10,
        out_specs=hbm,
        scratch=[
            zh,
            pltpu.VMEM((9 * W + 16, CELLS), BF16),
            tmp,
            pltpu.VMEM((9 * W, Q), F32),
            pltpu.VMEM((ncol * size, Q), BF16),
            pltpu.SemaphoreType.DMA((4,)),
        ],
    )(acc, inputs, hiddens[1], bh, hiddens[0], r0, r1, k0, k1, a)
    r0, r1 = swaps(p0, p1, "row")
    got = lax.all_to_all(send, "col", 0, 0, tiled=True)
    c0, c1 = corner(False, r0, r1, ql, qr)
    k0, k1 = swaps(c0, c1, "col")
    b, y = inside(a)
    got, c0, y = lax.optimization_barrier((got, c0, y))
    folded = call(functools.partial(fold_kernel, ncol), struct((Q, size), F32), in_specs=[whole()], out_specs=whole())(got)
    got = lax.all_to_all(folded, "row", 0, 0, tiled=True)
    y, folded = lax.optimization_barrier((y, folded))
    gi, grad_hidden, grad_cell = call(
        last_kernel,
        (struct((3,) + field, BF16), struct(field, F32), struct(field, F32)),
        in_specs=[whole()] * 9,
        out_specs=[whole()] * 3,
        scratch=[pltpu.VMEM((3 * Q, 3 * LANES), BF16), y3, tmp],
    )(gi1, gi2, dc, r0, r1, k0, k1, weights, y)
    count = Q // nrow // ncol
    grad_kernel, grad_bias = call(
        functools.partial(result_kernel, nrow),
        (struct((Q // nrow, size - 8), F32), struct((count, 1), F32)),
        in_specs=[whole()],
        out_specs=[whole()] * 2,
        scratch=[pltpu.VMEM((Q // nrow, LANES), F32)],
    )(got)
    return (gi, grad_hidden, grad_cell, grad_kernel, grad_bias.reshape(count))


def solution(mesh):
    placed = (
        P(None, None, "row", "col"),
        P(None, None, "row", "col"),
        P(None, None, "row", "col"),
        P(None, "row", "col"),
        P(None, "row", "col"),
        P("row", "col"),
        P(),
    )

    return jax.shard_map(
        shards,
        mesh=mesh,
        in_specs=placed,
        out_specs=(
            P(None, None, "row", "col"),
            P(None, "row", "col"),
            P(None, "row", "col"),
            P("row", "col"),
            P(("row", "col")),
        ),
        check_vma=False,
    )
```
